32 devices in a mesh: patch: 2 (over y), space: 4 (over z), tm: 2 (over x), row: 2 (over core).
Axes of the slice: x: 2, y: 2, z: 4, core: 2. Of those that a mesh axis runs over, the one named last changes fastest.
Arguments:
- doppler: float32 [32, 192, 256], P('tm', ('patch', 'space'), 'row'), parts along dimension 1, may hold values from -24 to 24
- cycle_masks: int32 [8, 33, 33], replicated, may hold values from 0 to 1, as said below
- lag_list: int32 [4], replicated, may hold values from 1 to 16, as said below
Outputs:
- correlations: float32 [2, 8, 4, 192, 256], P('tm', None, None, ('patch', 'space'), 'row'), parts along dimension 3
The draws below stay inside these ranges and needn't reach their ends.
There are 2 independent parts, one for each index of `patch`. The reference program is written for one: setup_inputs(seed, part) draws one part's arguments, and reference() takes and returns one part's arrays. A program takes and returns all parts, laid end to end along the dimension named above; an argument that names none is the same for every part. Nothing has to cross between parts.
Inputs may be any that keep to these rules, and one draw needn't show every extreme that they name: Each cycle_masks[r] is 1 only at offsets whose distance from the centre lies within half a pixel of one radius of 1 to 16, distinct radii over r, and is 1 at the offsets of that radius along both pixel directions; one annulus has radius 16. `lag_list`: the lags are distinct and one of them is 16.
All inputs are finite; a program needn't handle non-finite values.
Results may differ from the reference program's by a relative error of at most 0.0033.
Values may be sent and summed in bfloat16 or wider, within the bound.
No kernel may reach another device: no remote copies, remote signals or barrier semaphores. Data moves between devices by JAX's collectives and lax.ppermute only.
A program may use at most 64 MiB of HBM per device.

```python
import jax
import jax.numpy as jnp
from jax import lax

F_DEV = 16
RADII = 8
RMAX = 16
LAGS = 4
MAXLAG = 16
FRAMES = 32
COLS = 96
ROWS = 256
WINDOWS = 2


def cycle_radii(key):
    others = jax.random.permutation(jax.random.fold_in(key, 11), RMAX - 1)[:RADII - 1] + 1
    listed = jnp.concatenate([jnp.full((1,), RMAX, jnp.int32), others.astype(jnp.int32)])
    return listed[jax.random.permutation(jax.random.fold_in(key, 12), RADII)]


def draw_cycle_masks(key, part):
    radii = cycle_radii(key)
    width = 2 * RMAX + 1
    offset = jnp.arange(width, dtype=jnp.int32) - RMAX
    distance = 4 * (offset[:, None] * offset[:, None] + offset[None, :] * offset[None, :])
    lower = (2 * radii - 1) * (2 * radii - 1)
    upper = (2 * radii + 1) * (2 * radii + 1)
    inside = (distance[None] >= lower[:, None, None]) & (distance[None] < upper[:, None, None])
    keeping = jax.random.randint(jax.random.fold_in(key, 13), (RADII, width, width), 0, 4) > 0
    along_first = (offset[None, :, None] == radii[:, None, None]) & (offset[None, None, :] == 0)
    along_second = (offset[None, :, None] == 0) & (offset[None, None, :] == radii[:, None, None])
    return (inside & keeping | along_first | along_second).astype(jnp.int32)


def draw_lag_list(key, part):
    others = jax.random.permutation(jax.random.fold_in(key, 21), MAXLAG - 1)[:LAGS - 1] + 1
    listed = jnp.concatenate([jnp.full((1,), MAXLAG, jnp.int32), others.astype(jnp.int32)])
    return listed[jax.random.permutation(jax.random.fold_in(key, 22), LAGS)]


def block_scale(key, extent, cuts, smallest, top_value):
    def one(dim, shards_of):
        heights = jax.random.uniform(jax.random.fold_in(jax.random.fold_in(key, 6), dim), (shards_of,), jnp.float32, smallest / len(cuts), top_value / len(cuts))
        return jnp.repeat(jnp.exp(heights), extent[dim] // shards_of).reshape((-1,) + (1,) * (len(extent) - dim - 1))

    factor_of = one(*cuts[0])
    for cut in cuts[1:]:
        factor_of = factor_of * one(*cut)
    return factor_of


def scatter_about(own_key, dims, scale, bound, cuts=(), held_as=jnp.bfloat16):
    gain = block_scale(own_key, dims, cuts, -0.22, 0.18) if cuts else 1.0
    array = jax.random.normal(own_key, dims, jnp.float32) * scale * gain
    return jnp.minimum(jnp.maximum(array, -bound), bound).astype(held_as)


def setup_inputs(seed: int = 0, part: int = 0) -> dict:
    streams_of = jax.random.split(jax.random.key(seed), 4)
    part_keys = jax.random.split(jax.random.fold_in(streams_of[3], part), 4)
    doppler = scatter_about(part_keys[0], (FRAMES, COLS, ROWS), 4.0, 24.0, ((0, 2), (1, 4), (2, 2)), jnp.float32)
    cycle_masks = draw_cycle_masks(jax.random.fold_in(streams_of[3], 71), part)
    lag_list = draw_lag_list(jax.random.fold_in(streams_of[3], 71), part)
    return {"doppler": doppler, "cycle_masks": cycle_masks, "lag_list": lag_list}


gaussian_taps = (0.05448868, 0.24420134, 0.40261995, 0.24420134, 0.05448868)


def gaussian_blur(field, axis_dim, cell_count):
    summed = gaussian_taps[0] * lax.slice_in_dim(field, 0, cell_count, axis=axis_dim)
    for shift_index in range(1, len(gaussian_taps)):
        summed = summed + gaussian_taps[shift_index] * lax.slice_in_dim(field, shift_index, shift_index + cell_count, axis=axis_dim)
    return summed


def reference(doppler, cycle_masks, lag_list):
    blur_reach = len(gaussian_taps) // 2
    padded = jnp.pad(doppler, ((0, 0), (blur_reach, blur_reach), (blur_reach, blur_reach)))
    smooth = gaussian_blur(gaussian_blur(padded, 1, COLS), 2, ROWS).astype(jnp.bfloat16)
    kernel = cycle_masks.astype(jnp.float32)[:, None, :, :]
    counts = jnp.sum(cycle_masks, axis=(1, 2)).astype(jnp.float32)
    history = jnp.concatenate([jnp.zeros((MAXLAG, COLS, ROWS), smooth.dtype), smooth], 0)

    def window_corr(window_index):
        frame_start = (window_index * F_DEV).astype(jnp.int32)
        own_frames = lax.dynamic_slice_in_dim(smooth, frame_start, F_DEV, 0).astype(jnp.float32)
        cycle_sums = lax.conv_general_dilated(own_frames[:, None], kernel, (1, 1), ((RMAX, RMAX), (RMAX, RMAX)), dimension_numbers=("NCHW", "OIHW", "NCHW"), precision=lax.Precision.HIGHEST)
        annulus = cycle_sums / counts[None, :, None, None]
        earlier = jax.vmap(lambda lag_value: lax.dynamic_slice_in_dim(history, (MAXLAG + frame_start - lag_value).astype(jnp.int32), F_DEV, 0))(lag_list).astype(jnp.float32)
        return jnp.einsum("ltcx,trcx->rlcx", earlier, annulus, precision=lax.Precision.HIGHEST)

    return lax.map(window_corr, jnp.arange(WINDOWS, dtype=jnp.int32))
```

```python
import jax
import jax.numpy as jnp
from jax import lax
from jax.experimental import pallas as pl
from jax.experimental.pallas import tpu as pltpu
from jax.sharding import PartitionSpec as P

RMAX = 16
MAXLAG = 16
TILE = 32

gaussian_taps = (0.05448868, 0.24420134, 0.40261995, 0.24420134, 0.05448868)
REACH = len(gaussian_taps) // 2
LANES = 128
VMEM = pltpu.VMEM


def pairs(count, first):
    partner = list(range(count))
    for low in range(first, count - 1, 2):
        partner[low], partner[low + 1] = low + 1, low
    return [(source, target) for source, target in enumerate(partner)]


def onward(count):
    return [(source, (source + 1) % count) for source in range(count)]


def vmem_call(body, out_shape, scratch=(), smem=0, inputs=1, cost=None):
    specs = [pl.BlockSpec(memory_space=pltpu.SMEM)] * smem + [pl.BlockSpec(memory_space=VMEM)] * inputs
    many = isinstance(out_shape, (list, tuple))
    out_specs = [pl.BlockSpec(memory_space=VMEM)] * len(out_shape) if many else pl.BlockSpec(memory_space=VMEM)
    return pl.pallas_call(
        body,
        out_shape=out_shape,
        in_specs=specs,
        out_specs=out_specs,
        scratch_shapes=list(scratch),
        compiler_params=pltpu.CompilerParams(vmem_limit_bytes=24 * 1024 * 1024),
        cost_estimate=cost,
    )


def blend(parts):
    a, b, c, _, _ = gaussian_taps
    return c * parts[2] + b * (parts[1] + parts[3]) + a * (parts[0] + parts[4])


def table_body(flat_ref, table_ref, inverse_ref):
    radii, width = flat_ref.shape
    for r in range(radii):
        row = flat_ref[r : r + 1, :]
        total = jnp.sum(row, axis=1, keepdims=True)
        inverse_ref[r : r + 1, :] = jnp.broadcast_to(1.0 / total, (1, LANES))
        for k in range(width // LANES):
            wide = jnp.broadcast_to(row[:, k * LANES : (k + 1) * LANES], (TILE, LANES))
            turned = pltpu.roll(wide, 0, 1, stride=1, stride_axis=0)
            table_ref[r * TILE : (r + 1) * TILE, k * LANES : (k + 1) * LANES] = turned.astype(jnp.bfloat16)


def columns_body(frames, cols, x_ref, a_ref, b_ref, out_ref):
    place, count = lax.axis_index("space"), lax.axis_size("space")
    even = lax.rem(place, 2) == 0
    lowest, highest = place > 0, place < count - 1
    halo = RMAX + REACH

    def raw(c):
        if 0 <= c < cols:
            return x_ref[pl.ds(c, frames, stride=cols), :]
        at = c + cols if c < 0 else c - cols
        rows = pl.ds(at, frames, stride=cols)
        first, second, there = (b_ref, a_ref, lowest) if c < 0 else (a_ref, b_ref, highest)
        value = jnp.where(even, first[rows, :], second[rows, :])
        return jnp.where(there, value, jnp.zeros_like(value))

    held = {}
    for c in range(-halo, cols + halo):
        held[c] = raw(c)
        done = c - REACH
        if done >= -RMAX:
            out_ref[done + RMAX] = blend([held[done + k] for k in range(-REACH, REACH + 1)])


def rows_body(frames, cols, own_ref, low_ref, high_ref, tiles_ref, smooth_ref, turn_ref):
    place, count = lax.axis_index("row"), lax.axis_size("row")
    column, columns = lax.axis_index("space"), lax.axis_size("space")
    wide = cols + 2 * RMAX
    lane = lax.broadcasted_iota(jnp.int32, (frames, LANES), 1)
    halo = RMAX + REACH
    left = jnp.logical_and(lane >= LANES - halo, place > 0)
    right = jnp.logical_and(lane < halo, place < count - 1)
    left_kept = jnp.logical_and(lane >= LANES - RMAX, place > 0)
    right_kept = jnp.logical_and(lane < RMAX, place < count - 1)

    def around(near, far, k):
        if k == 0:
            return near
        near, far = pltpu.roll(near, (-k) % LANES, 1), pltpu.roll(far, (-k) % LANES, 1)
        return jnp.where(lane >= LANES - k if k > 0 else lane < -k, far, near)

    def smooth_of(c):
        own = own_ref[c]
        side = jnp.where(left, low_ref[c], jnp.where(right, high_ref[c], 0.0))
        shifts = range(-REACH, REACH + 1)
        main = blend([around(own, side, k) for k in shifts])
        edge = blend([around(side, own, k) for k in shifts])
        edge = jnp.where(jnp.logical_or(left_kept, right_kept), edge, 0.0)
        if c < RMAX or c >= RMAX + cols:
            inside = column > 0 if c < RMAX else column < columns - 1
            main, edge = jnp.where(inside, main, 0.0), jnp.where(inside, edge, 0.0)
        return main, edge

    tile_count = LANES // TILE
    first_half = lane < 2 * TILE

    def windows(c):
        main, edge = smooth_of(c)
        if RMAX <= c < RMAX + cols:
            turn_ref[(c - RMAX) * frames : (c - RMAX + 1) * frames, :] = main
        out = []
        for j in range(tile_count):
            start = TILE * j - RMAX
            source = main
            if start < 0:
                source = jnp.where(lane >= LANES + start, edge, main)
            if start + 2 * TILE > LANES:
                source = jnp.where(lane < start + 2 * TILE - LANES, edge, source)
            out.append((pltpu.roll(source, (-start) % LANES, 1), pltpu.roll(source, (2 * TILE - start) % LANES, 1)))
        return out

    before = windows(0)
    for c in range(wide):
        after = windows(c + 1) if c + 1 < wide else [(jnp.zeros((frames, LANES), jnp.float32),) * 2] * tile_count
        for j in range(tile_count):
            tiles_ref[j, c] = jnp.where(first_half, before[j][0], after[j][1]).astype(jnp.bfloat16)
        before = after
    for t in range(frames):
        smooth_ref[t] = turn_ref[pl.ds(t, cols, stride=frames), :].astype(jnp.bfloat16)


def sums_body(frames, cols, table_ref, tiles_ref, out_ref):
    tile_count = tiles_ref.shape[0]
    offsets = 2 * RMAX + 1
    rows = cols * frames
    for j in range(tile_count):
        pieces = []
        for a in range(0, offsets, 2):
            pieces.append(tiles_ref[j, a : a + cols].reshape(rows, LANES))
        stacked = jnp.concatenate(pieces, axis=1)
        found = lax.dot_general(
            stacked, table_ref[...], (((1,), (1,)), ((), ())), preferred_element_type=jnp.float32
        )
        for g in range(out_ref.shape[1]):
            out_ref[j, g] = found[:, g * LANES : (g + 1) * LANES]


def correlate_body(frames, cols, radii, lag_ref, sums_ref, own_ref, earlier_ref, inverse_ref, out_ref, spread_ref):
    lag_count = lag_ref.shape[0]
    tile_count = LANES // TILE
    wide = tile_count * LANES
    here = lax.broadcasted_iota(jnp.int32, (LANES, wide), 0)
    there = lax.broadcasted_iota(jnp.int32, (LANES, wide), 1)
    wanted = (there // LANES) * TILE + there % TILE
    pick = jnp.where(here == wanted, 1.0, 0.0).astype(jnp.bfloat16)
    begun = lax.axis_index("tm") > 0
    for half, source in enumerate((earlier_ref, own_ref)):
        value = jnp.dot(source[...], pick, preferred_element_type=jnp.float32)
        if half == 0:
            value = jnp.where(begun, value, 0.0)
        spread_ref[half * frames * cols : (half + 1) * frames * cols, :] = value
    lane = lax.broadcasted_iota(jnp.int32, (8, LANES), 1)
    block = [jnp.logical_and(lane >= TILE * j, lane < TILE * (j + 1)) for j in range(tile_count)]
    groups = radii * TILE // LANES
    per = LANES // TILE
    for c in range(0, cols, 8):
        totals = {}
        for j in range(tile_count):
            for t in range(frames):
                parts = [
                    sums_ref[j, g, pl.ds(c * frames + t, 8, stride=frames), :]
                    for g in range(groups)
                ]
                for lag in range(lag_count):
                    row = (MAXLAG + t - lag_ref[lag]) * cols + c
                    old = spread_ref[pl.ds(pl.multiple_of(row, 8), 8), j * LANES : (j + 1) * LANES]
                    for g in range(groups):
                        term = parts[g] * old
                        key = (lag, g, j)
                        totals[key] = totals[key] + term if key in totals else term
        for lag in range(lag_count):
            for g in range(groups):
                for q in range(per):
                    joined = None
                    for j in range(tile_count):
                        piece = totals[(lag, g, j)]
                        shift = (TILE * (j - q)) % LANES
                        piece = pltpu.roll(piece, shift, 1) if shift else piece
                        joined = piece if joined is None else jnp.where(block[j], piece, joined)
                    r = g * per + q
                    out_ref[r, lag, c : c + 8, :] = joined * inverse_ref[r : r + 1, :]


def local(doppler, cycle_masks, lag_list):
    frames, cols, rows = doppler.shape
    radii = cycle_masks.shape[0]
    lag_count = lag_list.shape[0]
    wide = cols + 2 * RMAX
    offsets = 2 * RMAX + 1
    tile_count = rows // TILE
    f32, bf16 = jnp.float32, jnp.bfloat16
    shape = jax.ShapeDtypeStruct

    flat = doppler.reshape(frames * cols, rows)
    count = lax.axis_size("space")
    one = lax.ppermute(flat, "space", pairs(count, 0))
    two = lax.ppermute(flat, "space", pairs(count, 1))

    kept = offsets + 1
    masks = jnp.pad(cycle_masks.astype(f32), ((0, 0), (0, kept - offsets), (0, 2 * TILE - offsets)))
    masks = masks.reshape(radii, kept * 2 * TILE)
    table, inverse = vmem_call(
        table_body, [shape((radii * TILE, kept * 2 * TILE), bf16), shape((radii, LANES), f32)]
    )(masks)

    def columns(*refs):
        columns_body(frames, cols, *refs)

    blurred = vmem_call(columns, shape((wide, frames, rows), f32), inputs=3)(flat, one, two)

    row_count = lax.axis_size("row")
    ring = onward(row_count)
    low = lax.ppermute(blurred, "row", ring)
    high = low if row_count == 2 else lax.ppermute(blurred, "row", [(b, a) for a, b in ring])

    def along(*refs):
        rows_body(frames, cols, *refs)

    tiles, smooth = vmem_call(
        along,
        [shape((tile_count, wide, frames, LANES), bf16), shape((frames, cols, rows), bf16)],
        scratch=[VMEM((cols * frames, LANES), f32)],
        inputs=3,
    )(blurred, low, high)

    smooth = smooth.reshape(frames * cols, rows)
    earlier = lax.ppermute(smooth, "tm", onward(lax.axis_size("tm")))

    def products(*refs):
        sums_body(frames, cols, *refs)

    flops = 2 * tile_count * cols * frames * radii * TILE * kept * 2 * TILE
    sums = vmem_call(
        products,
        shape((tile_count, radii * TILE // LANES, cols * frames, LANES), f32),
        inputs=2,
        cost=pl.CostEstimate(flops=flops, bytes_accessed=1 << 20, transcendentals=0),
    )(table, tiles)

    def correlate(*refs):
        correlate_body(frames, cols, radii, *refs)

    out = vmem_call(
        correlate,
        shape((radii, lag_count, cols, rows), f32),
        scratch=[VMEM((2 * frames * cols, tile_count * LANES), f32)],
        smem=1,
        inputs=4,
    )(lag_list, sums, smooth, earlier, inverse)
    return out[None]


def solution(mesh):
    return jax.shard_map(
        local,
        mesh=mesh,
        in_specs=(P("tm", ("patch", "space"), "row"), P(), P()),
        out_specs=P("tm", None, None, ("patch", "space"), "row"),
        check_vma=False,
    )
```

```python
import jax
import jax.numpy as jnp
from jax import lax
from jax.experimental import pallas as pl
from jax.experimental.pallas import tpu as pltpu
from jax.sharding import PartitionSpec as P

RMAX = 16
MAXLAG = 16
TILE = 32

gaussian_taps = (0.05448868, 0.24420134, 0.40261995, 0.24420134, 0.05448868)
REACH = len(gaussian_taps) // 2
LANES = 128
VMEM = pltpu.VMEM


def pairs(count, first, beside):
    partner = [None] * count
    for low in range(first, count - 1, 2):
        partner[low], partner[low + 1] = low + 1, low
    found = []
    for source, target in enumerate(partner):
        for other in range(beside):
            twin = other ^ 1 if (other ^ 1) < beside else other
            place = (source, twin) if target is None else (target, other)
            found.append((source * beside + other, place[0] * beside + place[1]))
    return found


def onward(count):
    return [(source, (source + 1) % count) for source in range(count)]


def vmem_call(body, out_shape, scratch=(), smem=0, inputs=1, cost=None):
    specs = [pl.BlockSpec(memory_space=pltpu.SMEM)] * smem + [pl.BlockSpec(memory_space=VMEM)] * inputs
    many = isinstance(out_shape, (list, tuple))
    out_specs = [pl.BlockSpec(memory_space=VMEM)] * len(out_shape) if many else pl.BlockSpec(memory_space=VMEM)
    return pl.pallas_call(
        body,
        out_shape=out_shape,
        in_specs=specs,
        out_specs=out_specs,
        scratch_shapes=list(scratch),
        compiler_params=pltpu.CompilerParams(vmem_limit_bytes=24 * 1024 * 1024),
        cost_estimate=cost,
    )


def blend(parts):
    a, b, c, _, _ = gaussian_taps
    return c * parts[2] + b * (parts[1] + parts[3]) + a * (parts[0] + parts[4])


def prepare_body(frames, cols, masks_ref, x_ref, table_ref, inverse_ref, blur_ref, turned_ref, wide_ref):
    offsets, radii, _ = masks_ref.shape
    span = 2 * TILE
    wide_ref[...] = jnp.zeros_like(wide_ref)
    wide_ref[0:offsets, :, 0:offsets] = masks_ref[...].astype(jnp.float32)
    total = jnp.zeros((radii, 1), jnp.float32)
    for k in range(wide_ref.shape[0] // 2):
        pair = wide_ref[2 * k] + pltpu.roll(wide_ref[2 * k + 1], span, 1)
        total = total + jnp.sum(pair, axis=1, keepdims=True)
        for r in range(radii):
            rows = jnp.broadcast_to(pair[r : r + 1, :], (TILE, LANES))
            turned = pltpu.roll(rows, 0, 1, stride=1, stride_axis=0)
            table_ref[r * TILE : (r + 1) * TILE, k * LANES : (k + 1) * LANES] = turned.astype(jnp.bfloat16)
    inverse_ref[...] = jnp.broadcast_to(1.0 / total, (radii, LANES))

    place, count = lax.axis_index("row"), lax.axis_size("row")
    source = lax.broadcasted_iota(jnp.int32, (LANES, LANES), 0)
    target = lax.broadcasted_iota(jnp.int32, (LANES, LANES), 1)
    outside = jnp.where(source < LANES // 2, source + LANES, source - LANES)

    def held(position):
        low = jnp.logical_or(position >= 0, place > 0)
        return jnp.logical_and(low, jnp.logical_or(position < LANES, place < count - 1))

    for n in range(blur_ref.shape[1] // LANES):
        if n < 2:
            landing = (target // span + 2 * n) * TILE - RMAX + target % span
        else:
            landing = target
        for half, origin in enumerate((source, outside)):
            apart = jnp.abs(origin - landing)
            weight = jnp.zeros((LANES, LANES), jnp.float32)
            for k in range(REACH + 1):
                weight = jnp.where(apart == k, gaussian_taps[REACH + k], weight)
            weight = jnp.where(jnp.logical_and(held(origin), held(landing)), weight, 0.0)
            blur_ref[half * LANES : (half + 1) * LANES, n * LANES : (n + 1) * LANES] = weight
    for c in range(cols):
        turned_ref[c] = x_ref[pl.ds(c, frames, stride=cols), :]


def columns_body(frames, cols, x_ref, a_ref, b_ref, out_ref):
    place, count = lax.axis_index("space"), lax.axis_size("space")
    even = lax.rem(place, 2) == 0
    lowest, highest = place > 0, place < count - 1
    halo = RMAX + REACH

    def raw(c):
        if 0 <= c < cols:
            return x_ref[c]
        at = c + cols if c < 0 else c - cols
        rows = pl.ds(at, frames, stride=cols)
        first, second, there = (b_ref, a_ref, lowest) if c < 0 else (a_ref, b_ref, highest)
        value = jnp.where(even, first[rows, :], second[rows, :])
        return jnp.where(there, value, jnp.zeros_like(value))

    held = {}
    for c in range(-halo, cols + halo):
        held[c] = raw(c)
        done = c - REACH
        if done >= -RMAX:
            value = blend([held[done + k] for k in range(-REACH, REACH + 1)])
            if done < 0 or done >= cols:
                value = jnp.where(lowest if done < 0 else highest, value, jnp.zeros_like(value))
            out_ref[(done + RMAX) * frames : (done + RMAX + 1) * frames, :] = value


def beside(low, high):
    if high is None:
        return low
    lane = lax.broadcasted_iota(jnp.int32, low.shape, 1)
    return jnp.where(lane < LANES // 2, high, low)


def exact_dot(x, y):
    return jnp.dot(x, y, precision=lax.Precision.HIGHEST, preferred_element_type=jnp.float32)


def own_body(frames, cols, own_ref, low_ref, high_ref, blur_ref, smooth_ref, turn_ref):
    rows = pl.ds(RMAX * frames, cols * frames)
    side = beside(low_ref[rows, :], None if high_ref is None else high_ref[rows, :])
    both = jnp.concatenate([own_ref[rows, :], side], axis=1)
    turn_ref[...] = exact_dot(both, blur_ref[:, 2 * LANES : 3 * LANES])
    for t in range(frames):
        smooth_ref[t * cols : (t + 1) * cols, :] = turn_ref[pl.ds(t, cols, stride=frames), :].astype(jnp.bfloat16)


def spread_of(smooth):
    wide = LANES // TILE * LANES
    here = lax.broadcasted_iota(jnp.int32, (LANES, wide), 0)
    there = lax.broadcasted_iota(jnp.int32, (LANES, wide), 1)
    wanted = (there // LANES) * TILE + there % TILE
    pick = jnp.where(here == wanted, 1.0, 0.0).astype(jnp.bfloat16)
    return jnp.dot(smooth, pick, preferred_element_type=jnp.float32)


def sums_body(frames, cols, own_ref, low_ref, high_ref, blur_ref, table_ref, smooth_ref, out_ref, spread_ref, tiles_ref, turn_ref):
    wide = cols + 2 * RMAX
    tile_count = LANES // TILE
    rows = cols * frames
    lane = lax.broadcasted_iota(jnp.int32, (frames, LANES), 1)
    first = lane < 2 * TILE
    chunk = 8
    before = None
    for start in range(0, wide + 1, chunk):
        if start < wide:
            part = pl.ds(start * frames, chunk * frames)
            side = beside(low_ref[part, :], None if high_ref is None else high_ref[part, :])
            both = jnp.concatenate([own_ref[part, :], side], axis=1)
            found = exact_dot(both, blur_ref[:, : 2 * LANES])
        for c in range(start, min(start + chunk, wide + 1)):
            now = []
            for n in range(tile_count // 2):
                if c < wide:
                    value = found[(c - start) * frames : (c - start + 1) * frames, n * LANES : (n + 1) * LANES]
                    now.append((value, pltpu.roll(value, 2 * TILE, 1)))
                else:
                    now.append((jnp.zeros((frames, LANES), jnp.float32),) * 2)
                if before is not None:
                    low = jnp.where(first, before[n][0], now[n][1])
                    high = jnp.where(first, before[n][1], now[n][0])
                    tiles_ref[2 * n, c - 1] = low.astype(jnp.bfloat16)
                    tiles_ref[2 * n + 1, c - 1] = high.astype(jnp.bfloat16)
            before = now
    spread_ref[...] = spread_of(smooth_ref[...])
    for j in range(tile_count):
        pieces = [tiles_ref[j, a : a + cols].reshape(rows, LANES) for a in range(0, 2 * RMAX + 1, 2)]
        found = lax.dot_general(
            jnp.concatenate(pieces, axis=1),
            table_ref[...],
            (((1,), (1,)), ((), ())),
            preferred_element_type=jnp.float32,
        )
        for g in range(out_ref.shape[1]):
            turn_ref[j, g] = found[:, g * LANES : (g + 1) * LANES]
            for t in range(frames):
                out_ref[j, g, t * cols : (t + 1) * cols, :] = turn_ref[j, g, pl.ds(t, cols, stride=frames), :]


def correlate_body(frames, cols, radii, lag_ref, sums_ref, own_ref, earlier_ref, inverse_ref, out_ref, spread_ref):
    lag_count = lag_ref.shape[0]
    tile_count = LANES // TILE
    begun = lax.axis_index("tm") > 0
    spread_ref[0 : frames * cols, :] = jnp.where(begun, spread_of(earlier_ref[...]), 0.0)
    spread_ref[frames * cols : 2 * frames * cols, :] = own_ref[...]
    lane = lax.broadcasted_iota(jnp.int32, (8, LANES), 1)
    block = [jnp.logical_and(lane >= TILE * j, lane < TILE * (j + 1)) for j in range(tile_count)]
    groups = radii * TILE // LANES
    per = LANES // TILE
    for c in range(0, cols, 8):
        totals = {}
        for j in range(tile_count):
            for t in range(frames):
                parts = [sums_ref[j, g, t * cols + c : t * cols + c + 8, :] for g in range(groups)]
                for lag in range(lag_count):
                    row = (MAXLAG + t - lag_ref[lag]) * cols + c
                    old = spread_ref[pl.ds(pl.multiple_of(row, 8), 8), j * LANES : (j + 1) * LANES]
                    for g in range(groups):
                        term = parts[g] * old
                        key = (lag, g, j)
                        totals[key] = totals[key] + term if key in totals else term
        for lag in range(lag_count):
            for g in range(groups):
                for q in range(per):
                    joined = None
                    for j in range(tile_count):
                        piece = totals[(lag, g, j)]
                        shift = (TILE * (j - q)) % LANES
                        piece = pltpu.roll(piece, shift, 1) if shift else piece
                        joined = piece if joined is None else jnp.where(block[j], piece, joined)
                    r = g * per + q
                    out_ref[r, lag, c : c + 8, :] = joined * inverse_ref[r : r + 1, :]


def local(doppler, cycle_masks, lag_list):
    frames, cols, rows = doppler.shape
    radii = cycle_masks.shape[0]
    lag_count = lag_list.shape[0]
    wide = cols + 2 * RMAX
    offsets = 2 * RMAX + 1
    tile_count = rows // TILE
    f32, bf16 = jnp.float32, jnp.bfloat16
    shape = jax.ShapeDtypeStruct

    flat = doppler.reshape(frames * cols, rows)
    count, row_count = lax.axis_size("space"), lax.axis_size("row")
    one = lax.ppermute(flat, ("space", "row"), pairs(count, 0, row_count))
    two = lax.ppermute(flat, ("space", "row"), pairs(count, 1, row_count))

    def prepare(*refs):
        prepare_body(frames, cols, *refs)

    depth = (offsets + 1) * 2 * TILE
    table, inverse, blur, turned = vmem_call(
        prepare,
        [
            shape((radii * TILE, depth), bf16),
            shape((radii, LANES), f32),
            shape((2 * LANES, 3 * LANES), f32),
            shape((cols, frames, LANES), f32),
        ],
        scratch=[VMEM((offsets + 1, radii, LANES), f32)],
        inputs=2,
    )(jnp.transpose(cycle_masks, (1, 0, 2)), flat)

    def columns(*refs):
        columns_body(frames, cols, *refs)

    blurred = vmem_call(columns, shape((wide * frames, rows), f32), inputs=3)(turned, one, two)

    ring = onward(row_count)
    low = lax.ppermute(blurred, "row", ring)
    sides = [low] if row_count == 2 else [low, lax.ppermute(blurred, "row", [(b, a) for a, b in ring])]

    def split(refs):
        return (refs[0], refs[1], refs[2] if len(sides) == 2 else None), refs[1 + len(sides) :]

    def own(*refs):
        lead, rest = split(refs)
        own_body(frames, cols, *lead, *rest)

    smooth = vmem_call(
        own, shape((frames * cols, rows), bf16), scratch=[VMEM((cols * frames, LANES), f32)], inputs=2 + len(sides)
    )(blurred, *sides, blur)
    earlier = lax.ppermute(smooth, "tm", onward(lax.axis_size("tm")))

    def products(*refs):
        lead, rest = split(refs)
        sums_body(frames, cols, *lead, *rest)

    groups = radii * TILE // LANES
    flops = 2 * tile_count * cols * frames * radii * TILE * depth
    sums, spread = vmem_call(
        products,
        [shape((tile_count, groups, frames * cols, LANES), f32), shape((frames * cols, tile_count * LANES), f32)],
        scratch=[
            VMEM((tile_count, wide, frames, LANES), bf16),
            VMEM((tile_count, groups, cols * frames, LANES), f32),
        ],
        inputs=4 + len(sides),
        cost=pl.CostEstimate(flops=flops, bytes_accessed=1 << 20, transcendentals=0),
    )(blurred, *sides, blur, table, smooth)

    def correlate(*refs):
        correlate_body(frames, cols, radii, *refs)

    out = vmem_call(
        correlate,
        shape((radii, lag_count, cols, rows), f32),
        scratch=[VMEM((2 * frames * cols, tile_count * LANES), f32)],
        smem=1,
        inputs=4,
    )(lag_list, sums, spread, earlier, inverse)
    return out[None]


def solution(mesh):
    return jax.shard_map(
        local,
        mesh=mesh,
        in_specs=(P("tm", ("patch", "space"), "row"), P(), P()),
        out_specs=P("tm", None, None, ("patch", "space"), "row"),
        check_vma=False,
    )
```

```python
import jax
import jax.numpy as jnp
from jax import lax
from jax.experimental import pallas as pl
from jax.experimental.pallas import tpu as pltpu
from jax.sharding import PartitionSpec as P


RMAX = 16
MAXLAG = 16
TILE = 32

gaussian_taps = (0.05448868, 0.24420134, 0.40261995, 0.24420134, 0.05448868)
REACH = len(gaussian_taps) // 2
LANES = 128
VMEM = pltpu.VMEM


def pairs(count, first, beside):
    partner = [None] * count
    for low in range(first, count - 1, 2):
        partner[low], partner[low + 1] = low + 1, low
    found = []
    for source, target in enumerate(partner):
        for other in range(beside):
            twin = other ^ 1 if (other ^ 1) < beside else other
            place = (source, twin) if target is None else (target, other)
            found.append((source * beside + other, place[0] * beside + place[1]))
    return found


def onward(count):
    return [(source, (source + 1) % count) for source in range(count)]


def vmem_call(body, out_shape, scratch=(), smem=0, inputs=1, cost=None, out_space=VMEM):
    specs = [pl.BlockSpec(memory_space=pltpu.SMEM)] * smem + [pl.BlockSpec(memory_space=VMEM)] * inputs
    many = isinstance(out_shape, (list, tuple))
    out_specs = pl.BlockSpec(memory_space=out_space)
    out_specs = [out_specs] * len(out_shape) if many else out_specs
    return pl.pallas_call(
        body,
        out_shape=out_shape,
        in_specs=specs,
        out_specs=out_specs,
        scratch_shapes=list(scratch),
        compiler_params=pltpu.CompilerParams(vmem_limit_bytes=24 * 1024 * 1024),
        cost_estimate=cost,
    )


def blend(parts):
    a, b, c, _, _ = gaussian_taps
    return c * parts[2] + b * (parts[1] + parts[3]) + a * (parts[0] + parts[4])


def prepare_body(frames, cols, masks_ref, x_ref, table_ref, inverse_ref, blur_ref, turned_ref, wide_ref):
    offsets, radii, _ = masks_ref.shape
    span = 2 * TILE
    wide_ref[...] = jnp.zeros_like(wide_ref)
    wide_ref[0:offsets, :, 0:offsets] = masks_ref[...].astype(jnp.float32)
    total = jnp.zeros((radii, 1), jnp.float32)
    for k in range(wide_ref.shape[0] // 2):
        pair = wide_ref[2 * k] + pltpu.roll(wide_ref[2 * k + 1], span, 1)
        total = total + jnp.sum(pair, axis=1, keepdims=True)
        for r in range(radii):
            rows = jnp.broadcast_to(pair[r : r + 1, :], (TILE, LANES))
            turned = pltpu.roll(rows, 0, 1, stride=1, stride_axis=0)
            table_ref[r * TILE : (r + 1) * TILE, k * LANES : (k + 1) * LANES] = turned.astype(jnp.bfloat16)
    inverse_ref[...] = jnp.broadcast_to(1.0 / total, (radii, LANES))

    place, count = lax.axis_index("row"), lax.axis_size("row")
    source = lax.broadcasted_iota(jnp.int32, (LANES, LANES), 0)
    target = lax.broadcasted_iota(jnp.int32, (LANES, LANES), 1)
    outside = jnp.where(source < LANES // 2, source + LANES, source - LANES)

    def held(position):
        low = jnp.logical_or(position >= 0, place > 0)
        return jnp.logical_and(low, jnp.logical_or(position < LANES, place < count - 1))

    for n in range(blur_ref.shape[1] // LANES):
        if n < 2:
            landing = (target // span + 2 * n) * TILE - RMAX + target % span
        else:
            landing = target
        for half, origin in enumerate((source, outside)):
            apart = jnp.abs(origin - landing)
            weight = jnp.zeros((LANES, LANES), jnp.float32)
            for k in range(REACH + 1):
                weight = jnp.where(apart == k, gaussian_taps[REACH + k], weight)
            weight = jnp.where(jnp.logical_and(held(origin), held(landing)), weight, 0.0)
            blur_ref[half * LANES : (half + 1) * LANES, n * LANES : (n + 1) * LANES] = weight
    for c in range(cols):
        turned_ref[c] = x_ref[pl.ds(c, frames, stride=cols), :]


def columns_body(frames, cols, x_ref, a_ref, b_ref, out_ref):
    place, count = lax.axis_index("space"), lax.axis_size("space")
    even = lax.rem(place, 2) == 0
    lowest, highest = place > 0, place < count - 1
    halo = RMAX + REACH

    def raw(c):
        if 0 <= c < cols:
            return x_ref[c]
        at = c + cols if c < 0 else c - cols
        rows = pl.ds(at, frames, stride=cols)
        first, second, there = (b_ref, a_ref, lowest) if c < 0 else (a_ref, b_ref, highest)
        value = jnp.where(even, first[rows, :], second[rows, :])
        return jnp.where(there, value, jnp.zeros_like(value))

    held = {}
    for c in range(-halo, cols + halo):
        held[c] = raw(c)
        done = c - REACH
        if done >= -RMAX:
            value = blend([held[done + k] for k in range(-REACH, REACH + 1)])
            if done < 0 or done >= cols:
                value = jnp.where(lowest if done < 0 else highest, value, jnp.zeros_like(value))
            out_ref[(done + RMAX) * frames : (done + RMAX + 1) * frames, :] = value


def beside(low, high):
    if high is None:
        return low
    lane = lax.broadcasted_iota(jnp.int32, low.shape, 1)
    return jnp.where(lane < LANES // 2, high, low)


def exact_dot(x, y):
    return jnp.dot(x, y, precision=lax.Precision.HIGHEST, preferred_element_type=jnp.float32)


def own_body(frames, cols, own_ref, low_ref, high_ref, blur_ref, smooth_ref, turn_ref):
    rows = pl.ds(RMAX * frames, cols * frames)
    side = beside(low_ref[rows, :], None if high_ref is None else high_ref[rows, :])
    both = jnp.concatenate([own_ref[rows, :], side], axis=1)
    turn_ref[...] = exact_dot(both, blur_ref[:, 2 * LANES : 3 * LANES])
    for t in range(frames):
        smooth_ref[t * cols : (t + 1) * cols, :] = turn_ref[pl.ds(t, cols, stride=frames), :].astype(jnp.bfloat16)


def spread_of(smooth):
    wide = LANES // TILE * LANES
    here = lax.broadcasted_iota(jnp.int32, (LANES, wide), 0)
    there = lax.broadcasted_iota(jnp.int32, (LANES, wide), 1)
    wanted = (there // LANES) * TILE + there % TILE
    pick = jnp.where(here == wanted, 1.0, 0.0).astype(jnp.bfloat16)
    return jnp.dot(smooth, pick, preferred_element_type=jnp.float32)


def sums_body(frames, cols, own_ref, low_ref, high_ref, blur_ref, table_ref, smooth_ref, out_ref, spread_ref, tiles_ref, turn_ref):
    wide = cols + 2 * RMAX
    tile_count = LANES // TILE
    rows = cols * frames
    lane = lax.broadcasted_iota(jnp.int32, (frames, LANES), 1)
    first = lane < 2 * TILE
    chunk = 8
    before = None
    for start in range(0, wide + 1, chunk):
        if start < wide:
            part = pl.ds(start * frames, chunk * frames)
            side = beside(low_ref[part, :], None if high_ref is None else high_ref[part, :])
            both = jnp.concatenate([own_ref[part, :], side], axis=1)
            found = exact_dot(both, blur_ref[:, : 2 * LANES])
        for c in range(start, min(start + chunk, wide + 1)):
            now = []
            for n in range(tile_count // 2):
                if c < wide:
                    value = found[(c - start) * frames : (c - start + 1) * frames, n * LANES : (n + 1) * LANES]
                    now.append((value, pltpu.roll(value, 2 * TILE, 1)))
                else:
                    now.append((jnp.zeros((frames, LANES), jnp.float32),) * 2)
                if before is not None:
                    low = jnp.where(first, before[n][0], now[n][1])
                    high = jnp.where(first, before[n][1], now[n][0])
                    tiles_ref[2 * n, c - 1] = low.astype(jnp.bfloat16)
                    tiles_ref[2 * n + 1, c - 1] = high.astype(jnp.bfloat16)
            before = now
    spread_ref[...] = spread_of(smooth_ref[...])
    for j in range(tile_count):
        pieces = [tiles_ref[j, a : a + cols].reshape(rows, LANES) for a in range(0, 2 * RMAX + 1, 2)]
        found = lax.dot_general(
            jnp.concatenate(pieces, axis=1),
            table_ref[...],
            (((1,), (1,)), ((), ())),
            preferred_element_type=jnp.float32,
        )
        for g in range(out_ref.shape[1]):
            turn_ref[j, g] = found[:, g * LANES : (g + 1) * LANES]
            for t in range(frames):
                out_ref[j, g, t * cols : (t + 1) * cols, :] = turn_ref[j, g, pl.ds(t, cols, stride=frames), :]


def correlate_body(frames, cols, radii, lag_ref, sums_ref, own_ref, earlier_ref, inverse_ref, out_ref, spread_ref, held_ref, sem):
    lag_count = lag_ref.shape[1]
    lags = [lag_ref[0, lag] for lag in range(lag_count)]
    tile_count = LANES // TILE
    begun = lax.axis_index("tm") > 0
    spread_ref[0 : frames * cols, :] = jnp.where(begun, spread_of(earlier_ref[...]), 0.0)
    spread_ref[frames * cols : 2 * frames * cols, :] = own_ref[...]
    lane = lax.broadcasted_iota(jnp.int32, (8, LANES), 1)
    block = [jnp.logical_and(lane >= TILE * j, lane < TILE * (j + 1)) for j in range(tile_count)]
    groups = radii * TILE // LANES
    per = LANES // TILE
    copies = []
    for c in range(0, cols, 8):
        totals = {}
        for j in range(tile_count):
            for t in range(frames):
                parts = [sums_ref[j, g, t * cols + c : t * cols + c + 8, :] for g in range(groups)]
                for lag in range(lag_count):
                    row = (MAXLAG + t - lags[lag]) * cols + c
                    old = spread_ref[pl.ds(pl.multiple_of(row, 8), 8), j * LANES : (j + 1) * LANES]
                    for g in range(groups):
                        term = parts[g] * old
                        key = (lag, g, j)
                        totals[key] = totals[key] + term if key in totals else term
        for lag in range(lag_count):
            for g in range(groups):
                for q in range(per):
                    joined = None
                    for j in range(tile_count):
                        piece = totals[(lag, g, j)]
                        shift = (TILE * (j - q)) % LANES
                        piece = pltpu.roll(piece, shift, 1) if shift else piece
                        joined = piece if joined is None else jnp.where(block[j], piece, joined)
                    r = g * per + q
                    held_ref[c // 8, r, lag] = joined * inverse_ref[r : r + 1, :]
        copies.append(pltpu.make_async_copy(held_ref.at[c // 8], out_ref.at[:, :, pl.ds(c, 8), :], sem.at[c // 8]))
        copies[-1].start()
    for copy in copies:
        copy.wait()


def local(doppler, cycle_masks, lag_list):
    frames, cols, rows = doppler.shape
    radii = cycle_masks.shape[0]
    lag_count = lag_list.shape[0]
    wide = cols + 2 * RMAX
    offsets = 2 * RMAX + 1
    tile_count = rows // TILE
    f32, bf16 = jnp.float32, jnp.bfloat16
    shape = jax.ShapeDtypeStruct

    flat = doppler.reshape(frames * cols, rows)
    count, row_count = lax.axis_size("space"), lax.axis_size("row")
    one = lax.ppermute(flat, ("space", "row"), pairs(count, 0, row_count))
    two = lax.ppermute(flat, ("space", "row"), pairs(count, 1, row_count))

    def prepare(*refs):
        prepare_body(frames, cols, *refs)

    depth = (offsets + 1) * 2 * TILE
    table, inverse, blur, turned = vmem_call(
        prepare,
        [
            shape((radii * TILE, depth), bf16),
            shape((radii, LANES), f32),
            shape((2 * LANES, 3 * LANES), f32),
            shape((cols, frames, LANES), f32),
        ],
        scratch=[VMEM((offsets + 1, radii, LANES), f32)],
        inputs=2,
    )(jnp.transpose(cycle_masks, (1, 0, 2)), flat)

    def columns(*refs):
        columns_body(frames, cols, *refs)

    blurred = vmem_call(columns, shape((wide * frames, rows), f32), inputs=3)(turned, one, two)

    ring = onward(row_count)
    low = lax.ppermute(blurred, "row", ring)
    sides = [low] if row_count == 2 else [low, lax.ppermute(blurred, "row", [(b, a) for a, b in ring])]

    def split(refs):
        return (refs[0], refs[1], refs[2] if len(sides) == 2 else None), refs[1 + len(sides) :]

    def own(*refs):
        lead, rest = split(refs)
        own_body(frames, cols, *lead, *rest)

    smooth = vmem_call(
        own, shape((frames * cols, rows), bf16), scratch=[VMEM((cols * frames, LANES), f32)], inputs=2 + len(sides)
    )(blurred, *sides, blur)
    earlier = lax.ppermute(smooth, "tm", onward(lax.axis_size("tm")))

    def products(*refs):
        lead, rest = split(refs)
        sums_body(frames, cols, *lead, *rest)

    groups = radii * TILE // LANES
    flops = 2 * tile_count * cols * frames * radii * TILE * depth
    sums, spread = vmem_call(
        products,
        [shape((tile_count, groups, frames * cols, LANES), f32), shape((frames * cols, tile_count * LANES), f32)],
        scratch=[
            VMEM((tile_count, wide, frames, LANES), bf16),
            VMEM((tile_count, groups, cols * frames, LANES), f32),
        ],
        inputs=4 + len(sides),
        cost=pl.CostEstimate(flops=flops, bytes_accessed=1 << 20, transcendentals=0),
    )(blurred, *sides, blur, table, smooth)

    def correlate(*refs):
        correlate_body(frames, cols, radii, *refs)

    out = vmem_call(
        correlate,
        shape((radii, lag_count, cols, rows), f32),
        scratch=[
            VMEM((2 * frames * cols, tile_count * LANES), f32),
            VMEM((cols // 8, radii, lag_count, 8, LANES), f32),
            pltpu.SemaphoreType.DMA((cols // 8,)),
        ],
        inputs=5,
        out_space=pl.ANY,
    )(lag_list.reshape(1, lag_count), sums, spread, earlier, inverse)
    return out[None]


def solution(mesh):
    return jax.shard_map(
        local,
        mesh=mesh,
        in_specs=(P("tm", ("patch", "space"), "row"), P(), P()),
        out_specs=P("tm", None, None, ("patch", "space"), "row"),
        check_vma=False,
    )
```

```python
import jax
import jax.numpy as jnp
from jax import lax
from jax.experimental import pallas as pl
from jax.experimental.pallas import tpu as pltpu
from jax.sharding import PartitionSpec as P


RMAX = 16
MAXLAG = 16
TILE = 32

gaussian_taps = (0.05448868, 0.24420134, 0.40261995, 0.24420134, 0.05448868)
REACH = len(gaussian_taps) // 2
LANES = 128
VMEM = pltpu.VMEM


def pairs(count, first, beside):
    partner = [None] * count
    for low in range(first, count - 1, 2):
        partner[low], partner[low + 1] = low + 1, low
    found = []
    for source, target in enumerate(partner):
        for other in range(beside):
            twin = other ^ 1 if (other ^ 1) < beside else other
            place = (source, twin) if target is None else (target, other)
            found.append((source * beside + other, place[0] * beside + place[1]))
    return found


def onward(count):
    return [(source, (source + 1) % count) for source in range(count)]


def vmem_call(body, out_shape, scratch=(), smem=0, inputs=1, cost=None, in_space=VMEM, out_space=VMEM, aliases=None):
    specs = [pl.BlockSpec(memory_space=pltpu.SMEM)] * smem + [pl.BlockSpec(memory_space=in_space)] * inputs
    many = isinstance(out_shape, (list, tuple))
    spaces = out_space if isinstance(out_space, list) else [out_space] * (len(out_shape) if many else 1)
    out_specs = [pl.BlockSpec(memory_space=space) for space in spaces]
    out_specs = out_specs if many else out_specs[0]
    return pl.pallas_call(
        body,
        out_shape=out_shape,
        in_specs=specs,
        out_specs=out_specs,
        scratch_shapes=list(scratch),
        compiler_params=pltpu.CompilerParams(vmem_limit_bytes=24 * 1024 * 1024),
        cost_estimate=cost,
        input_output_aliases=aliases or {},
    )


def blend(parts):
    a, b, c, _, _ = gaussian_taps
    return c * parts[2] + b * (parts[1] + parts[3]) + a * (parts[0] + parts[4])


def prepare_body(masks_hbm, x_hbm, table_ref, inverse_ref, blur_ref, x_ref, wide_ref, masks_ref, sem):
    masks_in = pltpu.make_async_copy(masks_hbm, masks_ref, sem.at[0])
    masks_in.start()
    x_in = pltpu.make_async_copy(x_hbm, x_ref, sem.at[1])
    x_in.start()
    offsets, radii, _ = masks_ref.shape
    span = 2 * TILE

    place, count = lax.axis_index("row"), lax.axis_size("row")
    source = lax.broadcasted_iota(jnp.int32, (LANES, LANES), 0)
    target = lax.broadcasted_iota(jnp.int32, (LANES, LANES), 1)
    outside = jnp.where(source < LANES // 2, source + LANES, source - LANES)

    def held(position):
        low = jnp.logical_or(position >= 0, place > 0)
        return jnp.logical_and(low, jnp.logical_or(position < LANES, place < count - 1))

    for n in range(blur_ref.shape[1] // LANES):
        landing = (target // span + 2 * n) * TILE - RMAX + target % span
        for half, origin in enumerate((source, outside)):
            apart = jnp.abs(origin - landing)
            weight = jnp.zeros((LANES, LANES), jnp.float32)
            for k in range(REACH + 1):
                weight = jnp.where(apart == k, gaussian_taps[REACH + k], weight)
            weight = jnp.where(jnp.logical_and(held(origin), held(landing)), weight, 0.0)
            blur_ref[half * LANES : (half + 1) * LANES, n * LANES : (n + 1) * LANES] = weight

    wide_ref[...] = jnp.zeros_like(wide_ref)
    masks_in.wait()
    wide_ref[0:offsets, :, 0:offsets] = masks_ref[...].astype(jnp.float32)
    total = jnp.zeros((radii, LANES), jnp.float32)
    for k in range(wide_ref.shape[0] // 2):
        pair = wide_ref[2 * k] + pltpu.roll(wide_ref[2 * k + 1], span, 1)
        total = total + pair
        for r in range(radii):
            rows = jnp.broadcast_to(pair[r : r + 1, :], (TILE, LANES))
            turned = pltpu.roll(rows, 0, 1, stride=1, stride_axis=0)
            table_ref[r * TILE : (r + 1) * TILE, k * LANES : (k + 1) * LANES] = turned.astype(jnp.bfloat16)
    inverse_ref[...] = jnp.broadcast_to(1.0 / jnp.sum(total, axis=1, keepdims=True), (radii, LANES))
    x_in.wait()


def beside(low, high):
    if high is None:
        return low
    lane = lax.broadcasted_iota(jnp.int32, low.shape, 1)
    return jnp.where(lane < LANES // 2, high, low)


def exact_dot(x, y):
    return jnp.dot(x, y, precision=lax.Precision.HIGHEST, preferred_element_type=jnp.float32)


def own_lanes(first, second):
    lane = lax.broadcasted_iota(jnp.int32, first.shape, 1)
    found = pltpu.roll(first, LANES - RMAX, 1)
    found = jnp.where(lane < TILE, found, pltpu.roll(first, LANES - RMAX - TILE, 1))
    found = jnp.where(lane < 2 * TILE, found, pltpu.roll(second, RMAX + TILE, 1))
    return jnp.where(lane < 3 * TILE, found, pltpu.roll(second, RMAX, 1))


def own_body(frames, cols, x_ref, low_ref, high_ref, blur_ref, smooth_ref, pairs_ref, rim_ref, both_ref, found_ref, turn_ref):
    inner = cols - 2 * REACH

    def raw(c):
        rows = pl.ds(c, frames, stride=cols)
        return x_ref[rows, :], beside(low_ref[rows, :], None if high_ref is None else high_ref[rows, :])

    held = {}
    for c in range(cols):
        held[c] = raw(c)
        done = c - REACH
        if done >= REACH:
            for n in range(2):
                both_ref[(done - REACH) * frames : (done - REACH + 1) * frames, n * LANES : (n + 1) * LANES] = blend(
                    [held[done + k][n] for k in range(-REACH, REACH + 1)]
                )
    found_ref[...] = exact_dot(both_ref[...], blur_ref[...])
    turn_ref[...] = jnp.zeros_like(turn_ref)
    lane = lax.broadcasted_iota(jnp.int32, (frames, LANES), 1)
    first = lane < 2 * TILE
    before = None
    for c in range(inner):
        rows = slice(c * frames, (c + 1) * frames)
        value = [found_ref[rows, n * LANES : (n + 1) * LANES] for n in range(2)]
        turn_ref[(c + REACH) * frames : (c + REACH + 1) * frames, :] = own_lanes(*value)
        now = [(v, pltpu.roll(v, 2 * TILE, 1)) for v in value]
        if c == 0 or c == inner - 1:
            for n in range(2):
                rim_ref[0 if c == 0 else 1, n] = value[n]
        if before is not None:
            for n in range(2):
                pairs_ref[2 * n, c - 1] = jnp.where(first, before[n][0], now[n][1]).astype(jnp.bfloat16)
                pairs_ref[2 * n + 1, c - 1] = jnp.where(first, before[n][1], now[n][0]).astype(jnp.bfloat16)
        before = now
    for t in range(frames):
        smooth_ref[t * cols : (t + 1) * cols, :] = turn_ref[pl.ds(t, cols, stride=frames), :].astype(jnp.bfloat16)


def columns_body(frames, cols, x_ref, a_ref, b_ref, out_ref, edge_ref):
    place, count = lax.axis_index("space"), lax.axis_size("space")
    even = lax.rem(place, 2) == 0
    lowest, highest = place > 0, place < count - 1
    halo = RMAX + REACH

    def raw(c):
        if 0 <= c < cols:
            return x_ref[pl.ds(c, frames, stride=cols), :]
        at = c + cols if c < 0 else c - cols
        rows = pl.ds(at, frames, stride=cols)
        first, second, there = (b_ref, a_ref, lowest) if c < 0 else (a_ref, b_ref, highest)
        value = jnp.where(even, first[rows, :], second[rows, :])
        return jnp.where(there, value, jnp.zeros_like(value))

    order = 0
    for low in (-halo, cols - 2 * REACH):
        held = {}
        for c in range(low, low + halo + 2 * REACH):
            held[c] = raw(c)
            done = c - REACH
            if done >= low + REACH:
                value = blend([held[done + k] for k in range(-REACH, REACH + 1)])
                if done < 0 or done >= cols:
                    value = jnp.where(lowest if done < 0 else highest, value, jnp.zeros_like(value))
                else:
                    slot = done if done < REACH else done - cols + 2 * REACH
                    edge_ref[slot * frames : (slot + 1) * frames, :] = value
                out_ref[order * frames : (order + 1) * frames, :] = value
                order += 1


def placed(frames, cols, edges):
    slots = 2 * REACH
    row = lax.broadcasted_iota(jnp.int32, (frames * cols, slots * frames), 0)
    from_row = lax.broadcasted_iota(jnp.int32, (frames * cols, slots * frames), 1)
    slot, frame = from_row // frames, from_row % frames
    column = jnp.where(slot < REACH, slot, slot + cols - slots)
    pick = jnp.where(row == frame * cols + column, 1.0, 0.0).astype(jnp.bfloat16)
    return jnp.dot(pick, edges, preferred_element_type=jnp.float32).astype(jnp.bfloat16)


def spread_of(smooth):
    wide = LANES // TILE * LANES
    here = lax.broadcasted_iota(jnp.int32, (LANES, wide), 0)
    there = lax.broadcasted_iota(jnp.int32, (LANES, wide), 1)
    wanted = (there // LANES) * TILE + there % TILE
    pick = jnp.where(here == wanted, 1.0, 0.0).astype(jnp.bfloat16)
    return jnp.dot(smooth, pick, preferred_element_type=jnp.float32)


def windows_body(frames, cols, own_ref, low_ref, high_ref, blur_ref, smooth_ref, pairs_ref, rim_ref, tiles_ref, whole_ref, found_ref):
    wide = cols + 2 * RMAX
    edge = RMAX + REACH
    lane = lax.broadcasted_iota(jnp.int32, (frames, LANES), 1)
    first = lane < 2 * TILE
    side = beside(low_ref[...], None if high_ref is None else high_ref[...])
    found_ref[...] = exact_dot(jnp.concatenate([own_ref[...], side], axis=1), blur_ref[...])

    def window(c, n):
        if c == wide:
            return jnp.zeros((frames, LANES), jnp.float32)
        if c == edge or c == wide - edge - 1:
            return rim_ref[0 if c == edge else 1, n]
        at = c if c < edge else c - wide + 2 * edge
        return found_ref[at * frames : (at + 1) * frames, n * LANES : (n + 1) * LANES]

    for begin, end in ((0, edge), (wide - edge - 1, wide)):
        before = None
        for c in range(begin, end + 1):
            now = []
            for n in range(2):
                value = window(c, n)
                now.append((value, pltpu.roll(value, 2 * TILE, 1)))
                if before is not None:
                    low = jnp.where(first, before[n][0], now[n][1])
                    high = jnp.where(first, before[n][1], now[n][0])
                    tiles_ref[2 * n, c - 1] = low.astype(jnp.bfloat16)
                    tiles_ref[2 * n + 1, c - 1] = high.astype(jnp.bfloat16)
            before = now
    for j in range(pairs_ref.shape[0]):
        tiles_ref[j, edge : wide - edge - 1] = pairs_ref[j]
    rows = slice(RMAX * frames, (RMAX + 2 * REACH) * frames)
    edges = own_lanes(found_ref[rows, 0:LANES], found_ref[rows, LANES : 2 * LANES]).astype(jnp.bfloat16)
    whole_ref[...] = smooth_ref[...] + placed(frames, cols, edges)


def sums_body(frames, cols, first, table_ref, tiles_ref, out_ref, turn_ref):
    rows = cols * frames
    for j in range(out_ref.shape[0]):
        pieces = [tiles_ref[first + j, a : a + cols].reshape(rows, LANES) for a in range(0, 2 * RMAX + 1, 2)]
        found = lax.dot_general(
            jnp.concatenate(pieces, axis=1),
            table_ref[...],
            (((1,), (1,)), ((), ())),
            preferred_element_type=jnp.float32,
        )
        for g in range(out_ref.shape[1]):
            turn_ref[j, g] = found[:, g * LANES : (g + 1) * LANES]
            for t in range(frames):
                out_ref[j, g, t * cols : (t + 1) * cols, :] = turn_ref[j, g, pl.ds(t, cols, stride=frames), :]


def later_body(frames, cols, first, table_ref, tiles_ref, whole_ref, earlier_ref, out_ref, spread_ref, turn_ref):
    begun = lax.axis_index("tm") > 0
    rows = frames * cols
    for half, source in enumerate((earlier_ref, whole_ref)):
        value = spread_of(source[...])
        if half == 0:
            value = jnp.where(begun, value, 0.0)
        for j in range(LANES // TILE):
            spread_ref[j, half * rows : (half + 1) * rows, :] = value[:, j * LANES : (j + 1) * LANES]
    sums_body(frames, cols, first, table_ref, tiles_ref, out_ref, turn_ref)


def correlate_body(
    frames, cols, radii, edge_ref, low_ref, high_ref, lag_ref, one_ref, two_ref, blur_ref, inverse_ref, given_ref,
    out_ref, spread_ref, held_ref, sem,
):
    lag_count = lag_ref.shape[1]
    lags = [lag_ref[0, lag] for lag in range(lag_count)]
    tile_count = LANES // TILE
    begun = lax.axis_index("tm") > 0
    del given_ref
    side = beside(low_ref[...], None if high_ref is None else high_ref[...])
    found = exact_dot(jnp.concatenate([edge_ref[...], side], axis=1), blur_ref[...])
    edges = own_lanes(found[:, :LANES], found[:, LANES : 2 * LANES]).astype(jnp.bfloat16)
    rims = jnp.where(begun, spread_of(edges), 0.0)
    for slot in range(2 * REACH):
        column = slot if slot < REACH else slot + cols - 2 * REACH
        for j in range(tile_count):
            value = rims[slot * frames : (slot + 1) * frames, j * LANES : (j + 1) * LANES]
            spread_ref[j, pl.ds(column, frames, stride=cols), :] = value
    lane = lax.broadcasted_iota(jnp.int32, (8, LANES), 1)
    block = [jnp.logical_and(lane >= TILE * j, lane < TILE * (j + 1)) for j in range(tile_count)]
    groups = radii * TILE // LANES
    per = LANES // TILE
    copies = []
    for c in range(0, cols, 8):
        totals = {}
        for j in range(tile_count):
            for t in range(frames):
                found_ref, at = (one_ref, j) if j < one_ref.shape[0] else (two_ref, j - one_ref.shape[0])
                parts = [found_ref[at, g, t * cols + c : t * cols + c + 8, :] for g in range(groups)]
                for lag in range(lag_count):
                    row = (MAXLAG + t - lags[lag]) * cols + c
                    old = spread_ref[j, pl.ds(pl.multiple_of(row, 8), 8), :]
                    for g in range(groups):
                        term = parts[g] * old
                        key = (lag, g, j)
                        totals[key] = totals[key] + term if key in totals else term
        for lag in range(lag_count):
            for g in range(groups):
                for q in range(per):
                    joined = None
                    for j in range(tile_count):
                        piece = totals[(lag, g, j)]
                        shift = (TILE * (j - q)) % LANES
                        piece = pltpu.roll(piece, shift, 1) if shift else piece
                        joined = piece if joined is None else jnp.where(block[j], piece, joined)
                    r = g * per + q
                    held_ref[c // 8, r, lag] = joined * inverse_ref[r : r + 1, :]
        copies.append(pltpu.make_async_copy(held_ref.at[c // 8], out_ref.at[:, :, pl.ds(c, 8), :], sem.at[c // 8]))
        copies[-1].start()
    for copy in copies:
        copy.wait()


def local(doppler, cycle_masks, lag_list):
    frames, cols, rows = doppler.shape
    radii = cycle_masks.shape[0]
    lag_count = lag_list.shape[0]
    wide = cols + 2 * RMAX
    edge = RMAX + REACH
    inner = cols - 2 * REACH
    offsets = 2 * RMAX + 1
    tile_count = rows // TILE
    groups = radii * TILE // LANES
    f32, bf16 = jnp.float32, jnp.bfloat16
    shape = jax.ShapeDtypeStruct

    flat = doppler.reshape(frames * cols, rows)
    count, row_count = lax.axis_size("space"), lax.axis_size("row")
    ring = onward(row_count)

    def across(value):
        low = lax.ppermute(value, "row", ring)
        return [low] if row_count == 2 else [low, lax.ppermute(value, "row", [(b, a) for a, b in ring])]

    def split(refs, lead=1):
        both = 1 if row_count == 2 else 2
        sides = (refs[lead], refs[lead + 1] if both == 2 else None)
        return refs[:lead] + sides + refs[lead + both :]

    one = lax.ppermute(flat, ("space", "row"), pairs(count, 0, row_count))
    two = lax.ppermute(flat, ("space", "row"), pairs(count, 1, row_count))
    near = across(flat)

    def prepare(*refs):
        prepare_body(*refs)

    depth = (offsets + 1) * 2 * TILE
    table, inverse, blur, held = vmem_call(
        prepare,
        [
            shape((radii * TILE, depth), bf16),
            shape((radii, LANES), f32),
            shape((2 * LANES, 2 * LANES), f32),
            shape((frames * cols, rows), f32),
        ],
        scratch=[
            VMEM((offsets + 1, radii, LANES), f32),
            VMEM((offsets, radii, offsets), jnp.int32),
            pltpu.SemaphoreType.DMA((2,)),
        ],
        inputs=2,
        in_space=pltpu.HBM,
    )(*[pltpu.with_memory_space_constraint(a, pltpu.HBM) for a in (jnp.transpose(cycle_masks, (1, 0, 2)), flat)])

    def own(*refs):
        own_body(frames, cols, *split(refs))

    smooth, inner_pairs, rim = vmem_call(
        own,
        [
            shape((frames * cols, rows), bf16),
            shape((tile_count, inner - 1, frames, LANES), bf16),
            shape((2, 2, frames, LANES), f32),
        ],
        scratch=[
            VMEM((inner * frames, 2 * LANES), f32),
            VMEM((inner * frames, 2 * LANES), f32),
            VMEM((cols * frames, LANES), f32),
        ],
        inputs=2 + len(near),
    )(held, *near, blur)
    later = onward(lax.axis_size("tm"))
    earlier = lax.ppermute(smooth, "tm", later)

    def columns(*refs):
        columns_body(frames, cols, *refs)

    blurred, edges = vmem_call(
        columns, [shape((2 * edge * frames, rows), f32), shape((2 * REACH * frames, rows), f32)], inputs=3
    )(held, one, two)

    sides = across(blurred)
    edges = lax.ppermute(edges, "tm", later)

    def windows(*refs):
        windows_body(frames, cols, *split(refs))

    tiles, whole = vmem_call(
        windows,
        [shape((tile_count, wide, frames, LANES), bf16), shape((frames * cols, rows), bf16)],
        scratch=[VMEM((2 * edge * frames, 2 * LANES), f32)],
        inputs=5 + len(sides),
    )(blurred, *sides, blur, smooth, inner_pairs, rim)

    half = tile_count // 2
    sums = shape((half, groups, frames * cols, LANES), f32)
    turn = VMEM((half, groups, cols * frames, LANES), f32)
    flops = tile_count * cols * frames * radii * TILE * depth
    cost = pl.CostEstimate(flops=flops, bytes_accessed=1 << 20, transcendentals=0)

    def products(*refs):
        sums_body(frames, cols, 0, *refs)

    first = vmem_call(products, sums, scratch=[turn], inputs=2, cost=cost)(table, tiles)

    far = across(edges)

    def others(*refs):
        later_body(frames, cols, half, *refs)

    second, spread = vmem_call(
        others,
        [sums, shape((tile_count, 2 * frames * cols, LANES), f32)],
        scratch=[turn],
        inputs=4,
        cost=cost,
    )(table, tiles, whole, earlier)

    def correlate(*refs):
        correlate_body(frames, cols, radii, *split(refs))

    out, _ = vmem_call(
        correlate,
        [shape((radii, lag_count, cols, rows), f32), shape(spread.shape, f32)],
        scratch=[
            VMEM((cols // 8, radii, lag_count, 8, LANES), f32),
            pltpu.SemaphoreType.DMA((cols // 8,)),
        ],
        inputs=7 + len(far),
        out_space=[pl.ANY, VMEM],
        aliases={6 + len(far): 1},
    )(edges, *far, lag_list.reshape(1, lag_count), first, second, blur, inverse, spread)
    return out[None]


def solution(mesh):
    return jax.shard_map(
        local,
        mesh=mesh,
        in_specs=(P("tm", ("patch", "space"), "row"), P(), P()),
        out_specs=P("tm", None, None, ("patch", "space"), "row"),
        check_vma=False,
    )
```

```python
import jax
import jax.numpy as jnp
from jax import lax
from jax.experimental import pallas as pl
from jax.experimental.pallas import tpu as pltpu
from jax.sharding import PartitionSpec as P


RMAX = 16
MAXLAG = 16
TILE = 32

gaussian_taps = (0.05448868, 0.24420134, 0.40261995, 0.24420134, 0.05448868)
REACH = len(gaussian_taps) // 2
LANES = 128
VMEM = pltpu.VMEM


def pairs(count, first, beside):
    partner = [None] * count
    for low in range(first, count - 1, 2):
        partner[low], partner[low + 1] = low + 1, low
    found = []
    for source, target in enumerate(partner):
        for other in range(beside):
            twin = other ^ 1 if (other ^ 1) < beside else other
            place = (source, twin) if target is None else (target, other)
            found.append((source * beside + other, place[0] * beside + place[1]))
    return found


def onward(count):
    return [(source, (source + 1) % count) for source in range(count)]


def vmem_call(body, out_shape, scratch=(), smem=0, inputs=1, cost=None, in_space=VMEM, out_space=VMEM, aliases=None):
    specs = [pl.BlockSpec(memory_space=pltpu.SMEM)] * smem + [pl.BlockSpec(memory_space=in_space)] * inputs
    many = isinstance(out_shape, (list, tuple))
    spaces = out_space if isinstance(out_space, list) else [out_space] * (len(out_shape) if many else 1)
    out_specs = [pl.BlockSpec(memory_space=space) for space in spaces]
    out_specs = out_specs if many else out_specs[0]
    return pl.pallas_call(
        body,
        out_shape=out_shape,
        in_specs=specs,
        out_specs=out_specs,
        scratch_shapes=list(scratch),
        compiler_params=pltpu.CompilerParams(vmem_limit_bytes=24 * 1024 * 1024),
        cost_estimate=cost,
        input_output_aliases=aliases or {},
    )


def blend(parts):
    a, b, c, _, _ = gaussian_taps
    return c * parts[2] + b * (parts[1] + parts[3]) + a * (parts[0] + parts[4])


def prepare_body(masks_hbm, x_hbm, blur_ref, x_ref, masks_ref, sem):
    copies = [
        pltpu.make_async_copy(x_hbm, x_ref, sem.at[0]),
        pltpu.make_async_copy(masks_hbm, masks_ref, sem.at[1]),
    ]
    for copy in copies:
        copy.start()
    span = 2 * TILE
    place, count = lax.axis_index("row"), lax.axis_size("row")
    source = lax.broadcasted_iota(jnp.int32, (LANES, LANES), 0)
    target = lax.broadcasted_iota(jnp.int32, (LANES, LANES), 1)
    outside = jnp.where(source < LANES // 2, source + LANES, source - LANES)

    def held(position):
        low = jnp.logical_or(position >= 0, place > 0)
        return jnp.logical_and(low, jnp.logical_or(position < LANES, place < count - 1))

    for n in range(blur_ref.shape[1] // LANES):
        landing = (target // span + 2 * n) * TILE - RMAX + target % span
        for half, origin in enumerate((source, outside)):
            apart = jnp.abs(origin - landing)
            weight = jnp.zeros((LANES, LANES), jnp.float32)
            for k in range(REACH + 1):
                weight = jnp.where(apart == k, gaussian_taps[REACH + k], weight)
            weight = jnp.where(jnp.logical_and(held(origin), held(landing)), weight, 0.0)
            blur_ref[half * LANES : (half + 1) * LANES, n * LANES : (n + 1) * LANES] = weight
    for copy in copies:
        copy.wait()


def table_body(masks_ref, table_ref, inverse_ref, wide_ref):
    offsets, radii, _ = masks_ref.shape
    wide_ref[...] = jnp.zeros_like(wide_ref)
    wide_ref[0:offsets, :, 0:offsets] = masks_ref[...].astype(jnp.float32)
    total = jnp.zeros((radii, LANES), jnp.float32)
    for k in range(wide_ref.shape[0] // 2):
        pair = wide_ref[2 * k] + pltpu.roll(wide_ref[2 * k + 1], 2 * TILE, 1)
        total = total + pair
        for r in range(radii):
            rows = jnp.broadcast_to(pair[r : r + 1, :], (TILE, LANES))
            turned = pltpu.roll(rows, 0, 1, stride=1, stride_axis=0)
            table_ref[r * TILE : (r + 1) * TILE, k * LANES : (k + 1) * LANES] = turned.astype(jnp.bfloat16)
    inverse_ref[...] = jnp.broadcast_to(1.0 / jnp.sum(total, axis=1, keepdims=True), (radii, LANES))


def beside(low, high):
    if high is None:
        return low
    lane = lax.broadcasted_iota(jnp.int32, low.shape, 1)
    return jnp.where(lane < LANES // 2, high, low)


def exact_dot(x, y):
    return jnp.dot(x, y, precision=lax.Precision.HIGHEST, preferred_element_type=jnp.float32)


def own_lanes(first, second):
    lane = lax.broadcasted_iota(jnp.int32, first.shape, 1)
    found = pltpu.roll(first, LANES - RMAX, 1)
    found = jnp.where(lane < TILE, found, pltpu.roll(first, LANES - RMAX - TILE, 1))
    found = jnp.where(lane < 2 * TILE, found, pltpu.roll(second, RMAX + TILE, 1))
    return jnp.where(lane < 3 * TILE, found, pltpu.roll(second, RMAX, 1))


def own_body(frames, cols, x_ref, low_ref, high_ref, blur_ref, smooth_ref, pairs_ref, rim_ref, both_ref, found_ref, turn_ref):
    inner = cols - 2 * REACH

    def raw(c):
        rows = pl.ds(c, frames, stride=cols)
        return x_ref[rows, :], beside(low_ref[rows, :], None if high_ref is None else high_ref[rows, :])

    held = {}
    for c in range(cols):
        held[c] = raw(c)
        done = c - REACH
        if done >= REACH:
            for n in range(2):
                both_ref[(done - REACH) * frames : (done - REACH + 1) * frames, n * LANES : (n + 1) * LANES] = blend(
                    [held[done + k][n] for k in range(-REACH, REACH + 1)]
                )
    found_ref[...] = exact_dot(both_ref[...], blur_ref[...])
    turn_ref[...] = jnp.zeros_like(turn_ref)
    lane = lax.broadcasted_iota(jnp.int32, (frames, LANES), 1)
    first = lane < 2 * TILE
    before = None
    for c in range(inner):
        rows = slice(c * frames, (c + 1) * frames)
        value = [found_ref[rows, n * LANES : (n + 1) * LANES] for n in range(2)]
        turn_ref[(c + REACH) * frames : (c + REACH + 1) * frames, :] = own_lanes(*value)
        now = [(v, pltpu.roll(v, 2 * TILE, 1)) for v in value]
        if c == 0 or c == inner - 1:
            for n in range(2):
                rim_ref[0 if c == 0 else 1, n] = value[n]
        if before is not None:
            for n in range(2):
                pairs_ref[2 * n, c - 1] = jnp.where(first, before[n][0], now[n][1]).astype(jnp.bfloat16)
                pairs_ref[2 * n + 1, c - 1] = jnp.where(first, before[n][1], now[n][0]).astype(jnp.bfloat16)
        before = now
    for t in range(frames):
        smooth_ref[t * cols : (t + 1) * cols, :] = turn_ref[pl.ds(t, cols, stride=frames), :].astype(jnp.bfloat16)


def columns_body(frames, cols, x_ref, a_ref, b_ref, out_ref, edge_ref):
    place, count = lax.axis_index("space"), lax.axis_size("space")
    even = lax.rem(place, 2) == 0
    lowest, highest = place > 0, place < count - 1
    halo = RMAX + REACH

    def raw(c):
        if 0 <= c < cols:
            return x_ref[pl.ds(c, frames, stride=cols), :]
        at = c + cols if c < 0 else c - cols
        rows = pl.ds(at, frames, stride=cols)
        first, second, there = (b_ref, a_ref, lowest) if c < 0 else (a_ref, b_ref, highest)
        value = jnp.where(even, first[rows, :], second[rows, :])
        return jnp.where(there, value, jnp.zeros_like(value))

    order = 0
    for low in (-halo, cols - 2 * REACH):
        held = {}
        for c in range(low, low + halo + 2 * REACH):
            held[c] = raw(c)
            done = c - REACH
            if done >= low + REACH:
                value = blend([held[done + k] for k in range(-REACH, REACH + 1)])
                if done < 0 or done >= cols:
                    value = jnp.where(lowest if done < 0 else highest, value, jnp.zeros_like(value))
                else:
                    slot = done if done < REACH else done - cols + 2 * REACH
                    edge_ref[slot * frames : (slot + 1) * frames, :] = value
                out_ref[order * frames : (order + 1) * frames, :] = value
                order += 1


def placed(frames, cols, edges):
    slots = 2 * REACH
    row = lax.broadcasted_iota(jnp.int32, (frames * cols, slots * frames), 0)
    from_row = lax.broadcasted_iota(jnp.int32, (frames * cols, slots * frames), 1)
    slot, frame = from_row // frames, from_row % frames
    column = jnp.where(slot < REACH, slot, slot + cols - slots)
    pick = jnp.where(row == frame * cols + column, 1.0, 0.0).astype(jnp.bfloat16)
    return jnp.dot(pick, edges, preferred_element_type=jnp.float32).astype(jnp.bfloat16)


def spread_of(smooth):
    wide = LANES // TILE * LANES
    here = lax.broadcasted_iota(jnp.int32, (LANES, wide), 0)
    there = lax.broadcasted_iota(jnp.int32, (LANES, wide), 1)
    wanted = (there // LANES) * TILE + there % TILE
    pick = jnp.where(here == wanted, 1.0, 0.0).astype(jnp.bfloat16)
    return jnp.dot(smooth, pick, preferred_element_type=jnp.float32)


def windows_body(frames, cols, own_ref, low_ref, high_ref, blur_ref, smooth_ref, pairs_ref, rim_ref, tiles_ref, whole_ref, found_ref):
    wide = cols + 2 * RMAX
    edge = RMAX + REACH
    lane = lax.broadcasted_iota(jnp.int32, (frames, LANES), 1)
    first = lane < 2 * TILE
    side = beside(low_ref[...], None if high_ref is None else high_ref[...])
    found_ref[...] = exact_dot(jnp.concatenate([own_ref[...], side], axis=1), blur_ref[...])

    def window(c, n):
        if c == wide:
            return jnp.zeros((frames, LANES), jnp.float32)
        if c == edge or c == wide - edge - 1:
            return rim_ref[0 if c == edge else 1, n]
        at = c if c < edge else c - wide + 2 * edge
        return found_ref[at * frames : (at + 1) * frames, n * LANES : (n + 1) * LANES]

    for begin, end in ((0, edge), (wide - edge - 1, wide)):
        before = None
        for c in range(begin, end + 1):
            now = []
            for n in range(2):
                value = window(c, n)
                now.append((value, pltpu.roll(value, 2 * TILE, 1)))
                if before is not None:
                    low = jnp.where(first, before[n][0], now[n][1])
                    high = jnp.where(first, before[n][1], now[n][0])
                    tiles_ref[2 * n, c - 1] = low.astype(jnp.bfloat16)
                    tiles_ref[2 * n + 1, c - 1] = high.astype(jnp.bfloat16)
            before = now
    for j in range(pairs_ref.shape[0]):
        tiles_ref[j, edge : wide - edge - 1] = pairs_ref[j]
    rows = slice(RMAX * frames, (RMAX + 2 * REACH) * frames)
    edges = own_lanes(found_ref[rows, 0:LANES], found_ref[rows, LANES : 2 * LANES]).astype(jnp.bfloat16)
    whole_ref[...] = smooth_ref[...] + placed(frames, cols, edges)


def sums_body(frames, cols, first, table_ref, tiles_ref, out_ref):
    rows, pitch = cols * frames, frames + 8
    for j in range(out_ref.shape[0]):
        pieces = [tiles_ref[first + j, a : a + cols].reshape(rows, LANES) for a in range(0, 2 * RMAX + 1, 2)]
        found = lax.dot_general(
            jnp.concatenate(pieces, axis=1),
            table_ref[...],
            (((1,), (1,)), ((), ())),
            preferred_element_type=jnp.float32,
        )
        for g in range(out_ref.shape[1]):
            for c in range(cols):
                value = found[c * frames : (c + 1) * frames, g * LANES : (g + 1) * LANES]
                out_ref[j, g, c * pitch : c * pitch + frames, :] = value


def correlate_block(frames, cols, n, lags, sources, spread_ref, inverse_ref, total_ref, held):
    groups, pitch, per = total_ref.shape[2], frames + 8, LANES // TILE
    tile_count = len(sources)
    lane = lax.broadcasted_iota(jnp.int32, (8, LANES), 1)
    block = [jnp.logical_and(lane >= TILE * j, lane < TILE * (j + 1)) for j in range(tile_count)]
    c = n * 8
    for j, (found_ref, at) in enumerate(sources):
        totals = {}
        for t in range(frames):
            parts = [found_ref[at, g, pl.ds(c * pitch + t, 8, stride=pitch), :] for g in range(groups)]
            for lag in range(len(lags)):
                row = (MAXLAG - lags[lag]) * cols + c + t * cols
                old = spread_ref[j, pl.ds(pl.multiple_of(row, 8), 8), :]
                for g in range(groups):
                    term = parts[g] * old
                    key = (lag, g)
                    totals[key] = totals[key] + term if key in totals else term
        for lag in range(len(lags)):
            for g in range(groups):
                total_ref[j, lag, g] = totals[(lag, g)]
    for lag in range(len(lags)):
        for g in range(groups):
            pieces = [total_ref[j, lag, g] for j in range(tile_count)]
            for q in range(per):
                joined = None
                for j in range(tile_count):
                    shift = (TILE * (j - q)) % LANES
                    piece = pltpu.roll(pieces[j], shift, 1) if shift else pieces[j]
                    joined = piece if joined is None else jnp.where(block[j], piece, joined)
                r = g * per + q
                held[r, lag] = joined * inverse_ref[r : r + 1, :]


def read_lags(lag_ref):
    return [lag_ref[0, lag] for lag in range(lag_ref.shape[1])]


def later_body(
    frames, cols, table_ref, tiles_ref, whole_ref, earlier_ref, lag_ref, inverse_ref, early_ref,
    out_ref, spread_ref, held_ref, total_ref,
):
    begun = lax.axis_index("tm") > 0
    rows, done = frames * cols, early_ref.shape[0]
    for half, source in enumerate((earlier_ref, whole_ref)):
        value = spread_of(source[...])
        if half == 0:
            value = jnp.where(begun, value, 0.0)
        for j in range(LANES // TILE):
            spread_ref[j, half * rows : (half + 1) * rows, :] = value[:, j * LANES : (j + 1) * LANES]
    sums_body(frames, cols, done, table_ref, tiles_ref, out_ref)
    sources = [(early_ref, j) for j in range(done)] + [(out_ref, j) for j in range(out_ref.shape[0])]
    lags = read_lags(lag_ref)
    for n in range(held_ref.shape[0]):
        correlate_block(frames, cols, n + 1, lags, sources, spread_ref, inverse_ref, total_ref, held_ref.at[n])


def correlate_body(
    frames, cols, edge_ref, low_ref, high_ref, lag_ref, early_ref, late_ref, middle_ref, inverse_ref, given_ref,
    out_ref, spread_ref, held_ref, total_ref, sem,
):
    del given_ref
    blocks = cols // 8

    def send(source, n):
        rows = pl.ds(pl.multiple_of(n * 8, 8), 8)
        return pltpu.make_async_copy(source, out_ref.at[:, :, rows, :], sem.at[n])

    for n in range(blocks - 2):
        send(middle_ref.at[n], n + 1).start()
    tile_count = LANES // TILE
    begun = lax.axis_index("tm") > 0
    side = beside(low_ref[...], None if high_ref is None else high_ref[...])
    place, count = lax.axis_index("row"), lax.axis_size("row")
    spot = lax.broadcasted_iota(jnp.int32, side.shape, 1)
    halo = spot < LANES // 2
    there = jnp.logical_or(jnp.logical_and(halo, place < count - 1), jnp.logical_and(jnp.logical_not(halo), place > 0))
    side = jnp.where(there, side, 0.0)
    shifted = []
    for k in range(-REACH, REACH + 1):
        near, far = edge_ref[...], side
        if k:
            near, far = pltpu.roll(near, (-k) % LANES, 1), pltpu.roll(far, (-k) % LANES, 1)
            near = jnp.where(spot >= LANES - k if k > 0 else spot < -k, far, near)
        shifted.append(near)
    rims = jnp.where(begun, blend(shifted).astype(jnp.bfloat16).astype(jnp.float32), 0.0)
    for j in range(tile_count):
        tile = jnp.where(jnp.logical_and(spot >= TILE * j, spot < TILE * (j + 1)), rims, 0.0)
        shift = TILE
        while shift < LANES:
            tile = tile + pltpu.roll(tile, shift, 1)
            shift *= 2
        for slot in range(2 * REACH):
            column = slot if slot < REACH else slot + cols - 2 * REACH
            spread_ref[j, pl.ds(column, frames, stride=cols), :] = tile[slot * frames : (slot + 1) * frames, :]
    sources = [(early_ref, j) for j in range(early_ref.shape[0])] + [(late_ref, j) for j in range(late_ref.shape[0])]
    lags = read_lags(lag_ref)

    def one_end(end, carry):
        n = end * (blocks - 1)
        correlate_block(frames, cols, n, lags, sources, spread_ref, inverse_ref, total_ref, held_ref.at[end])
        send(held_ref.at[end], n).start()
        return carry

    lax.fori_loop(0, 2, one_end, 0)
    for n in range(blocks):
        send(held_ref.at[0], n).wait()


def local(doppler, cycle_masks, lag_list):
    frames, cols, rows = doppler.shape
    radii = cycle_masks.shape[0]
    lag_count = lag_list.shape[0]
    wide = cols + 2 * RMAX
    edge = RMAX + REACH
    inner = cols - 2 * REACH
    offsets = 2 * RMAX + 1
    tile_count = rows // TILE
    groups = radii * TILE // LANES
    f32, bf16 = jnp.float32, jnp.bfloat16
    shape = jax.ShapeDtypeStruct

    flat = doppler.reshape(frames * cols, rows)
    count, row_count = lax.axis_size("space"), lax.axis_size("row")
    ring = onward(row_count)

    def across(value):
        low = lax.ppermute(value, "row", ring)
        return [low] if row_count == 2 else [low, lax.ppermute(value, "row", [(b, a) for a, b in ring])]

    def split(refs, lead=1):
        both = 1 if row_count == 2 else 2
        sides = (refs[lead], refs[lead + 1] if both == 2 else None)
        return refs[:lead] + sides + refs[lead + both :]

    one = lax.ppermute(flat, ("space", "row"), pairs(count, 0, row_count))
    two = lax.ppermute(flat, ("space", "row"), pairs(count, 1, row_count))
    near = across(flat)

    depth = (offsets + 1) * 2 * TILE
    masks = jnp.transpose(cycle_masks, (1, 0, 2))
    blur, held, masks = vmem_call(
        prepare_body,
        [
            shape((2 * LANES, 2 * LANES), f32),
            shape((frames * cols, rows), f32),
            shape((offsets, radii, offsets), jnp.int32),
        ],
        scratch=[pltpu.SemaphoreType.DMA((2,))],
        inputs=2,
        in_space=pltpu.HBM,
    )(*[pltpu.with_memory_space_constraint(value, pltpu.HBM) for value in (masks, flat)])

    def own(*refs):
        own_body(frames, cols, *split(refs))

    smooth, inner_pairs, rim = vmem_call(
        own,
        [
            shape((frames * cols, rows), bf16),
            shape((tile_count, inner - 1, frames, LANES), bf16),
            shape((2, 2, frames, LANES), f32),
        ],
        scratch=[
            VMEM((inner * frames, 2 * LANES), f32),
            VMEM((inner * frames, 2 * LANES), f32),
            VMEM((cols * frames, LANES), f32),
        ],
        inputs=2 + len(near),
    )(held, *near, blur)
    later = onward(lax.axis_size("tm"))
    earlier = lax.ppermute(smooth, "tm", later)

    table, inverse = vmem_call(
        table_body,
        [shape((radii * TILE, depth), bf16), shape((radii, LANES), f32)],
        scratch=[VMEM((offsets + 1, radii, LANES), f32)],
    )(masks)

    def columns(*refs):
        columns_body(frames, cols, *refs)

    blurred, edges = vmem_call(
        columns, [shape((2 * edge * frames, rows), f32), shape((2 * REACH * frames, rows), f32)], inputs=3
    )(held, one, two)

    sides = across(blurred)
    edges = lax.ppermute(edges, "tm", later)

    def windows(*refs):
        windows_body(frames, cols, *split(refs))

    tiles, whole = vmem_call(
        windows,
        [shape((tile_count, wide, frames, LANES), bf16), shape((frames * cols, rows), bf16)],
        scratch=[VMEM((2 * edge * frames, 2 * LANES), f32)],
        inputs=5 + len(sides),
    )(blurred, *sides, blur, smooth, inner_pairs, rim)

    blocks = cols // 8
    total = VMEM((tile_count, lag_count, groups, 8, LANES), f32)
    lags = lag_list.reshape(1, lag_count)

    def sums_of(count):
        flops = 2 * count * cols * frames * radii * TILE * depth
        cost = pl.CostEstimate(flops=flops, bytes_accessed=1 << 20, transcendentals=0)
        return shape((count, groups, cols * (frames + 8), LANES), f32), cost

    def products(*refs):
        sums_body(frames, cols, 0, *refs)

    sums, cost = sums_of(tile_count - 1)
    early = vmem_call(products, sums, inputs=2, cost=cost)(table, tiles)

    far = across(edges)

    def others(*refs):
        later_body(frames, cols, *refs)

    sums, cost = sums_of(1)
    late, spread, middle = vmem_call(
        others,
        [
            sums,
            shape((tile_count, 2 * frames * cols, LANES), f32),
            shape((blocks - 2, radii, lag_count, 8, LANES), f32),
        ],
        scratch=[total],
        inputs=7,
        cost=cost,
    )(table, tiles, whole, earlier, lags, inverse, early)

    def correlate(*refs):
        correlate_body(frames, cols, *split(refs))

    out, _ = vmem_call(
        correlate,
        [shape((radii, lag_count, cols, rows), f32), shape(spread.shape, f32)],
        scratch=[
            VMEM((2, radii, lag_count, 8, LANES), f32),
            total,
            pltpu.SemaphoreType.DMA((blocks,)),
        ],
        inputs=7 + len(far),
        out_space=[pl.ANY, VMEM],
        aliases={6 + len(far): 1},
    )(edges, *far, lags, early, late, middle, inverse, spread)
    return out[None]


def solution(mesh):
    return jax.shard_map(
        local,
        mesh=mesh,
        in_specs=(P("tm", ("patch", "space"), "row"), P(), P()),
        out_specs=P("tm", None, None, ("patch", "space"), "row"),
        check_vma=False,
    )
```

```python
import jax
import jax.numpy as jnp
from jax import lax
from jax.experimental import pallas as pl
from jax.experimental.pallas import tpu as pltpu
from jax.sharding import PartitionSpec as P


RMAX = 16
MAXLAG = 16
TILE = 32

gaussian_taps = (0.05448868, 0.24420134, 0.40261995, 0.24420134, 0.05448868)
REACH = len(gaussian_taps) // 2
LANES = 128
VMEM = pltpu.VMEM
PHASES = 3


def pairs(count, first, beside):
    partner = [None] * count
    for low in range(first, count - 1, PHASES):
        partner[low], partner[low + 1] = low + 1, low
    found = []
    for source, target in enumerate(partner):
        for other in range(beside):
            twin = other ^ 1 if (other ^ 1) < beside else other
            place = (source, twin) if target is None else (target, other)
            found.append((source * beside + other, place[0] * beside + place[1]))
    return found


def onward(count):
    return [(source, (source + 1) % count) for source in range(count)]


def vmem_call(body, out_shape, scratch=(), smem=0, inputs=1, cost=None, in_space=VMEM, out_space=VMEM, aliases=None):
    specs = [pl.BlockSpec(memory_space=pltpu.SMEM)] * smem + [pl.BlockSpec(memory_space=in_space)] * inputs
    many = isinstance(out_shape, (list, tuple))
    spaces = out_space if isinstance(out_space, list) else [out_space] * (len(out_shape) if many else 1)
    out_specs = [pl.BlockSpec(memory_space=space) for space in spaces]
    out_specs = out_specs if many else out_specs[0]
    return pl.pallas_call(
        body,
        out_shape=out_shape,
        in_specs=specs,
        out_specs=out_specs,
        scratch_shapes=list(scratch),
        compiler_params=pltpu.CompilerParams(vmem_limit_bytes=24 * 1024 * 1024),
        cost_estimate=cost,
        input_output_aliases=aliases or {},
    )


def blend(parts):
    a, b, c, _, _ = gaussian_taps
    return c * parts[2] + b * (parts[1] + parts[3]) + a * (parts[0] + parts[4])


def prepare_body(masks_hbm, x_hbm, blur_ref, x_ref, masks_ref, sem):
    copies = [
        pltpu.make_async_copy(x_hbm, x_ref, sem.at[0]),
        pltpu.make_async_copy(masks_hbm, masks_ref, sem.at[1]),
    ]
    for copy in copies:
        copy.start()
    span = 2 * TILE
    place, count = lax.axis_index("row"), lax.axis_size("row")
    source = lax.broadcasted_iota(jnp.int32, (LANES, LANES), 0)
    target = lax.broadcasted_iota(jnp.int32, (LANES, LANES), 1)
    outside = jnp.where(source < LANES // 2, source + LANES, source - LANES)

    def held(position):
        low = jnp.logical_or(position >= 0, place > 0)
        return jnp.logical_and(low, jnp.logical_or(position < LANES, place < count - 1))

    for n in range(blur_ref.shape[1] // LANES):
        landing = (target // span + 2 * n) * TILE - RMAX + target % span
        for half, origin in enumerate((source, outside)):
            apart = jnp.abs(origin - landing)
            weight = jnp.zeros((LANES, LANES), jnp.float32)
            for k in range(REACH + 1):
                weight = jnp.where(apart == k, gaussian_taps[REACH + k], weight)
            weight = jnp.where(jnp.logical_and(held(origin), held(landing)), weight, 0.0)
            blur_ref[half * LANES : (half + 1) * LANES, n * LANES : (n + 1) * LANES] = weight
    for copy in copies:
        copy.wait()


def table_body(masks_ref, table_ref, inverse_ref, wide_ref, pair_ref):
    offsets, radii, _ = masks_ref.shape
    wide_ref[...] = jnp.zeros_like(wide_ref)
    wide_ref[0:offsets, :, 0:offsets] = masks_ref[...].astype(jnp.float32)
    total = jnp.zeros((radii, LANES), jnp.float32)
    count = wide_ref.shape[0] // 2
    for k in range(count):
        pair = wide_ref[2 * k] + pltpu.roll(wide_ref[2 * k + 1], 2 * TILE, 1)
        total = total + pair
        pair_ref[k * radii : (k + 1) * radii, :] = pair
    for k in range(count):
        for r in range(radii):
            rows = pair_ref[pl.ds(k * radii + r, TILE, stride=0), :]
            turned = pltpu.roll(rows, 0, 1, stride=1, stride_axis=0)
            table_ref[r * TILE : (r + 1) * TILE, k * LANES : (k + 1) * LANES] = turned.astype(jnp.bfloat16)
    inverse_ref[...] = jnp.broadcast_to(1.0 / jnp.sum(total, axis=1, keepdims=True), (radii, LANES))


def beside(low, high):
    if high is None:
        return low
    lane = lax.broadcasted_iota(jnp.int32, low.shape, 1)
    return jnp.where(lane < LANES // 2, high, low)


def exact_dot(x, y):
    return jnp.dot(x, y, precision=lax.Precision.HIGHEST, preferred_element_type=jnp.float32)


def own_lanes(first, second):
    lane = lax.broadcasted_iota(jnp.int32, first.shape, 1)
    found = pltpu.roll(first, LANES - RMAX, 1)
    found = jnp.where(lane < TILE, found, pltpu.roll(first, LANES - RMAX - TILE, 1))
    found = jnp.where(lane < 2 * TILE, found, pltpu.roll(second, RMAX + TILE, 1))
    return jnp.where(lane < 3 * TILE, found, pltpu.roll(second, RMAX, 1))


def own_body(frames, cols, x_ref, low_ref, high_ref, blur_ref, smooth_ref, pairs_ref, rim_ref, both_ref, found_ref, turn_ref):
    inner = cols - 2 * REACH

    def raw(c):
        rows = pl.ds(c, frames, stride=cols)
        return x_ref[rows, :], beside(low_ref[rows, :], None if high_ref is None else high_ref[rows, :])

    held = {}
    for c in range(cols):
        held[c] = raw(c)
        done = c - REACH
        if done >= REACH:
            for n in range(2):
                both_ref[(done - REACH) * frames : (done - REACH + 1) * frames, n * LANES : (n + 1) * LANES] = blend(
                    [held[done + k][n] for k in range(-REACH, REACH + 1)]
                )
    found_ref[...] = exact_dot(both_ref[...], blur_ref[...])
    turn_ref[...] = jnp.zeros_like(turn_ref)
    lane = lax.broadcasted_iota(jnp.int32, (frames, LANES), 1)
    first = lane < 2 * TILE
    before = None
    for c in range(inner):
        rows = slice(c * frames, (c + 1) * frames)
        value = [found_ref[rows, n * LANES : (n + 1) * LANES] for n in range(2)]
        turn_ref[(c + REACH) * frames : (c + REACH + 1) * frames, :] = own_lanes(*value)
        now = [(v, pltpu.roll(v, 2 * TILE, 1)) for v in value]
        if c == 0 or c == inner - 1:
            for n in range(2):
                rim_ref[0 if c == 0 else 1, n] = value[n]
        if before is not None:
            for n in range(2):
                pairs_ref[2 * n, c - 1] = jnp.where(first, before[n][0], now[n][1]).astype(jnp.bfloat16)
                pairs_ref[2 * n + 1, c - 1] = jnp.where(first, before[n][1], now[n][0]).astype(jnp.bfloat16)
        before = now
    for t in range(frames):
        smooth_ref[t * cols : (t + 1) * cols, :] = turn_ref[pl.ds(t, cols, stride=frames), :].astype(jnp.bfloat16)


def columns_body(frames, cols, x_ref, a_ref, b_ref, c_ref, out_ref, edge_ref):
    place, count = lax.axis_index("space"), lax.axis_size("space")
    phase = lax.rem(place, PHASES)
    lowest, highest = place > 0, place < count - 1
    halo = RMAX + REACH

    def raw(c):
        if 0 <= c < cols:
            return x_ref[pl.ds(c, frames, stride=cols), :]
        at = c + cols if c < 0 else c - cols
        rows = pl.ds(at, frames, stride=cols)
        refs, there = ((c_ref, a_ref, b_ref), lowest) if c < 0 else ((a_ref, b_ref, c_ref), highest)
        value = jnp.where(phase == 0, refs[0][rows, :], jnp.where(phase == 1, refs[1][rows, :], refs[2][rows, :]))
        return jnp.where(there, value, jnp.zeros_like(value))

    order = 0
    for low in (-halo, cols - 2 * REACH):
        held = {}
        for c in range(low, low + halo + 2 * REACH):
            held[c] = raw(c)
            done = c - REACH
            if done >= low + REACH:
                value = blend([held[done + k] for k in range(-REACH, REACH + 1)])
                if done < 0 or done >= cols:
                    value = jnp.where(lowest if done < 0 else highest, value, jnp.zeros_like(value))
                else:
                    slot = done if done < REACH else done - cols + 2 * REACH
                    edge_ref[slot * frames : (slot + 1) * frames, :] = value
                out_ref[order * frames : (order + 1) * frames, :] = value
                order += 1


def placed(frames, cols, edges):
    slots = 2 * REACH
    row = lax.broadcasted_iota(jnp.int32, (frames * cols, slots * frames), 0)
    from_row = lax.broadcasted_iota(jnp.int32, (frames * cols, slots * frames), 1)
    slot, frame = from_row // frames, from_row % frames
    column = jnp.where(slot < REACH, slot, slot + cols - slots)
    pick = jnp.where(row == frame * cols + column, 1.0, 0.0).astype(jnp.bfloat16)
    return jnp.dot(pick, edges, preferred_element_type=jnp.float32).astype(jnp.bfloat16)


def spread_of(smooth):
    wide = LANES // TILE * LANES
    here = lax.broadcasted_iota(jnp.int32, (LANES, wide), 0)
    there = lax.broadcasted_iota(jnp.int32, (LANES, wide), 1)
    wanted = (there // LANES) * TILE + there % TILE
    pick = jnp.where(here == wanted, 1.0, 0.0).astype(jnp.bfloat16)
    return jnp.dot(smooth, pick, preferred_element_type=jnp.float32)


def windows_body(frames, cols, own_ref, low_ref, high_ref, blur_ref, smooth_ref, pairs_ref, rim_ref, tiles_ref, whole_ref, found_ref):
    wide = cols + 2 * RMAX
    edge = RMAX + REACH
    lane = lax.broadcasted_iota(jnp.int32, (frames, LANES), 1)
    first = lane < 2 * TILE
    side = beside(low_ref[...], None if high_ref is None else high_ref[...])
    found_ref[...] = exact_dot(jnp.concatenate([own_ref[...], side], axis=1), blur_ref[...])

    def window(c, n):
        if c == wide:
            return jnp.zeros((frames, LANES), jnp.float32)
        if c == edge or c == wide - edge - 1:
            return rim_ref[0 if c == edge else 1, n]
        at = c if c < edge else c - wide + 2 * edge
        return found_ref[at * frames : (at + 1) * frames, n * LANES : (n + 1) * LANES]

    for begin, end in ((0, edge), (wide - edge - 1, wide)):
        before = None
        for c in range(begin, end + 1):
            now = []
            for n in range(2):
                value = window(c, n)
                now.append((value, pltpu.roll(value, 2 * TILE, 1)))
                if before is not None:
                    low = jnp.where(first, before[n][0], now[n][1])
                    high = jnp.where(first, before[n][1], now[n][0])
                    tiles_ref[2 * n, c - 1] = low.astype(jnp.bfloat16)
                    tiles_ref[2 * n + 1, c - 1] = high.astype(jnp.bfloat16)
            before = now
    for j in range(pairs_ref.shape[0]):
        tiles_ref[j, edge : wide - edge - 1] = pairs_ref[j]
    rows = slice(RMAX * frames, (RMAX + 2 * REACH) * frames)
    edges = own_lanes(found_ref[rows, 0:LANES], found_ref[rows, LANES : 2 * LANES]).astype(jnp.bfloat16)
    whole_ref[...] = smooth_ref[...] + placed(frames, cols, edges)


def sums_body(frames, cols, first, table_ref, tiles_ref, out_ref):
    rows, pitch = cols * frames, frames + 8
    for j in range(out_ref.shape[0]):
        pieces = [tiles_ref[first + j, a : a + cols].reshape(rows, LANES) for a in range(0, 2 * RMAX + 1, 2)]
        found = lax.dot_general(
            jnp.concatenate(pieces, axis=1),
            table_ref[...],
            (((1,), (1,)), ((), ())),
            preferred_element_type=jnp.float32,
        )
        for g in range(out_ref.shape[1]):
            for c in range(cols):
                value = found[c * frames : (c + 1) * frames, g * LANES : (g + 1) * LANES]
                out_ref[j, g, c * pitch : c * pitch + frames, :] = value


def correlate_block(frames, cols, n, lags, sources, spread_ref, inverse_ref, total_ref, held):
    groups, pitch, per = total_ref.shape[2], frames + 8, LANES // TILE
    tile_count = len(sources)
    lane = lax.broadcasted_iota(jnp.int32, (8, LANES), 1)
    block = [jnp.logical_and(lane >= TILE * j, lane < TILE * (j + 1)) for j in range(tile_count)]
    c = n * 8
    for j, (found_ref, at) in enumerate(sources):
        totals = {}
        for t in range(frames):
            parts = [found_ref[at, g, pl.ds(c * pitch + t, 8, stride=pitch), :] for g in range(groups)]
            for lag in range(len(lags)):
                row = (MAXLAG - lags[lag]) * cols + c + t * cols
                old = spread_ref[j, pl.ds(pl.multiple_of(row, 8), 8), :]
                for g in range(groups):
                    term = parts[g] * old
                    key = (lag, g)
                    totals[key] = totals[key] + term if key in totals else term
        for lag in range(len(lags)):
            for g in range(groups):
                total_ref[j, lag, g] = totals[(lag, g)]
    for lag in range(len(lags)):
        for g in range(groups):
            pieces = [total_ref[j, lag, g] for j in range(tile_count)]
            for q in range(per):
                joined = None
                for j in range(tile_count):
                    shift = (TILE * (j - q)) % LANES
                    piece = pltpu.roll(pieces[j], shift, 1) if shift else pieces[j]
                    joined = piece if joined is None else jnp.where(block[j], piece, joined)
                r = g * per + q
                held[r, lag] = joined * inverse_ref[r : r + 1, :]


def read_lags(lag_ref):
    return [lag_ref[0, lag] for lag in range(lag_ref.shape[1])]


def later_body(
    frames, cols, table_ref, tiles_ref, whole_ref, earlier_ref, lag_ref, inverse_ref, early_ref,
    out_ref, spread_ref, held_ref, total_ref,
):
    begun = lax.axis_index("tm") > 0
    rows, done = frames * cols, early_ref.shape[0]
    for half, source in enumerate((earlier_ref, whole_ref)):
        value = spread_of(source[...])
        if half == 0:
            value = jnp.where(begun, value, 0.0)
        for j in range(LANES // TILE):
            spread_ref[j, half * rows : (half + 1) * rows, :] = value[:, j * LANES : (j + 1) * LANES]
    sums_body(frames, cols, done, table_ref, tiles_ref, out_ref)
    sources = [(early_ref, j) for j in range(done)] + [(out_ref, j) for j in range(out_ref.shape[0])]
    lags = read_lags(lag_ref)
    for n in range(held_ref.shape[0]):
        correlate_block(frames, cols, n + 1, lags, sources, spread_ref, inverse_ref, total_ref, held_ref.at[n])


def correlate_body(
    frames, cols, edge_ref, low_ref, high_ref, lag_ref, early_ref, late_ref, middle_ref, inverse_ref, given_ref,
    out_ref, spread_ref, held_ref, total_ref, sem,
):
    del given_ref
    blocks = cols // 8

    def send(source, n):
        rows = pl.ds(pl.multiple_of(n * 8, 8), 8)
        return pltpu.make_async_copy(source, out_ref.at[:, :, rows, :], sem.at[n])

    for n in range(blocks - 2):
        send(middle_ref.at[n], n + 1).start()
    tile_count = LANES // TILE
    begun = lax.axis_index("tm") > 0
    side = beside(low_ref[...], None if high_ref is None else high_ref[...])
    place, count = lax.axis_index("row"), lax.axis_size("row")
    spot = lax.broadcasted_iota(jnp.int32, side.shape, 1)
    halo = spot < LANES // 2
    there = jnp.logical_or(jnp.logical_and(halo, place < count - 1), jnp.logical_and(jnp.logical_not(halo), place > 0))
    side = jnp.where(there, side, 0.0)
    shifted = []
    for k in range(-REACH, REACH + 1):
        near, far = edge_ref[...], side
        if k:
            near, far = pltpu.roll(near, (-k) % LANES, 1), pltpu.roll(far, (-k) % LANES, 1)
            near = jnp.where(spot >= LANES - k if k > 0 else spot < -k, far, near)
        shifted.append(near)
    rims = jnp.where(begun, blend(shifted).astype(jnp.bfloat16).astype(jnp.float32), 0.0)
    for j in range(tile_count):
        tile = jnp.where(jnp.logical_and(spot >= TILE * j, spot < TILE * (j + 1)), rims, 0.0)
        shift = TILE
        while shift < LANES:
            tile = tile + pltpu.roll(tile, shift, 1)
            shift *= 2
        for slot in range(2 * REACH):
            column = slot if slot < REACH else slot + cols - 2 * REACH
            spread_ref[j, pl.ds(column, frames, stride=cols), :] = tile[slot * frames : (slot + 1) * frames, :]
    sources = [(early_ref, j) for j in range(early_ref.shape[0])] + [(late_ref, j) for j in range(late_ref.shape[0])]
    lags = read_lags(lag_ref)

    def one_end(end, carry):
        n = end * (blocks - 1)
        correlate_block(frames, cols, n, lags, sources, spread_ref, inverse_ref, total_ref, held_ref.at[end])
        send(held_ref.at[end], n).start()
        return carry

    lax.fori_loop(0, 2, one_end, 0)
    for n in range(blocks):
        send(held_ref.at[0], n).wait()


def local(doppler, cycle_masks, lag_list):
    frames, cols, rows = doppler.shape
    radii = cycle_masks.shape[0]
    lag_count = lag_list.shape[0]
    wide = cols + 2 * RMAX
    edge = RMAX + REACH
    inner = cols - 2 * REACH
    offsets = 2 * RMAX + 1
    tile_count = rows // TILE
    groups = radii * TILE // LANES
    f32, bf16 = jnp.float32, jnp.bfloat16
    shape = jax.ShapeDtypeStruct

    flat = doppler.reshape(frames * cols, rows)
    count, row_count = lax.axis_size("space"), lax.axis_size("row")
    ring = onward(row_count)

    def across(value):
        low = lax.ppermute(value, "row", ring)
        return [low] if row_count == 2 else [low, lax.ppermute(value, "row", [(b, a) for a, b in ring])]

    def split(refs, lead=1):
        both = 1 if row_count == 2 else 2
        sides = (refs[lead], refs[lead + 1] if both == 2 else None)
        return refs[:lead] + sides + refs[lead + both :]

    one = lax.ppermute(flat, ("space", "row"), pairs(count, 0, row_count))
    two = lax.ppermute(flat, ("space", "row"), pairs(count, 1, row_count))
    three = lax.ppermute(flat, ("space", "row"), pairs(count, 2, row_count))
    near = across(flat)

    depth = (offsets + 1) * 2 * TILE
    masks = jnp.transpose(cycle_masks, (1, 0, 2))
    blur, held, masks = vmem_call(
        prepare_body,
        [
            shape((2 * LANES, 2 * LANES), f32),
            shape((frames * cols, rows), f32),
            shape((offsets, radii, offsets), jnp.int32),
        ],
        scratch=[pltpu.SemaphoreType.DMA((2,))],
        inputs=2,
        in_space=pltpu.HBM,
    )(*[pltpu.with_memory_space_constraint(value, pltpu.HBM) for value in (masks, flat)])

    def own(*refs):
        own_body(frames, cols, *split(refs))

    smooth, inner_pairs, rim = vmem_call(
        own,
        [
            shape((frames * cols, rows), bf16),
            shape((tile_count, inner - 1, frames, LANES), bf16),
            shape((2, 2, frames, LANES), f32),
        ],
        scratch=[
            VMEM((inner * frames, 2 * LANES), f32),
            VMEM((inner * frames, 2 * LANES), f32),
            VMEM((cols * frames, LANES), f32),
        ],
        inputs=2 + len(near),
    )(held, *near, blur)
    later = onward(lax.axis_size("tm"))
    earlier = lax.ppermute(smooth, "tm", later)

    table, inverse = vmem_call(
        table_body,
        [shape((radii * TILE, depth), bf16), shape((radii, LANES), f32)],
        scratch=[VMEM((offsets + 1, radii, LANES), f32), VMEM(((offsets + 1) // 2 * radii, LANES), f32)],
    )(masks)

    def columns(*refs):
        columns_body(frames, cols, *refs)

    blurred, edges = vmem_call(
        columns, [shape((2 * edge * frames, rows), f32), shape((2 * REACH * frames, rows), f32)], inputs=4
    )(held, one, two, three)

    sides = across(blurred)
    edges = lax.ppermute(edges, "tm", later)

    def windows(*refs):
        windows_body(frames, cols, *split(refs))

    tiles, whole = vmem_call(
        windows,
        [shape((tile_count, wide, frames, LANES), bf16), shape((frames * cols, rows), bf16)],
        scratch=[VMEM((2 * edge * frames, 2 * LANES), f32)],
        inputs=5 + len(sides),
    )(blurred, *sides, blur, smooth, inner_pairs, rim)

    blocks = cols // 8
    total = VMEM((tile_count, lag_count, groups, 8, LANES), f32)
    lags = lag_list.reshape(1, lag_count)

    def sums_of(count):
        flops = 2 * count * cols * frames * radii * TILE * depth
        cost = pl.CostEstimate(flops=flops, bytes_accessed=1 << 20, transcendentals=0)
        return shape((count, groups, cols * (frames + 8), LANES), f32), cost

    def products(*refs):
        sums_body(frames, cols, 0, *refs)

    sums, cost = sums_of(tile_count - 1)
    early = vmem_call(products, sums, inputs=2, cost=cost)(table, tiles)

    far = across(edges)

    def others(*refs):
        later_body(frames, cols, *refs)

    sums, cost = sums_of(1)
    late, spread, middle = vmem_call(
        others,
        [
            sums,
            shape((tile_count, 2 * frames * cols, LANES), f32),
            shape((blocks - 2, radii, lag_count, 8, LANES), f32),
        ],
        scratch=[total],
        inputs=7,
        cost=cost,
    )(table, tiles, whole, earlier, lags, inverse, early)

    def correlate(*refs):
        correlate_body(frames, cols, *split(refs))

    out, _ = vmem_call(
        correlate,
        [shape((radii, lag_count, cols, rows), f32), shape(spread.shape, f32)],
        scratch=[
            VMEM((2, radii, lag_count, 8, LANES), f32),
            total,
            pltpu.SemaphoreType.DMA((blocks,)),
        ],
        inputs=7 + len(far),
        out_space=[pl.ANY, VMEM],
        aliases={6 + len(far): 1},
    )(edges, *far, lags, early, late, middle, inverse, spread)
    return out[None]


def solution(mesh):
    return jax.shard_map(
        local,
        mesh=mesh,
        in_specs=(P("tm", ("patch", "space"), "row"), P(), P()),
        out_specs=P("tm", None, None, ("patch", "space"), "row"),
        check_vma=False,
    )
```

```python
import jax
import jax.numpy as jnp
from jax import lax
from jax.experimental import pallas as pl
from jax.experimental.pallas import tpu as pltpu
from jax.sharding import PartitionSpec as P


RMAX = 16
MAXLAG = 16
TILE = 32

gaussian_taps = (0.05448868, 0.24420134, 0.40261995, 0.24420134, 0.05448868)
REACH = len(gaussian_taps) // 2
LANES = 128
VMEM = pltpu.VMEM
PHASES = 3


def pairs(count, first, beside):
    partner = [None] * count
    for low in range(first, count - 1, PHASES):
        partner[low], partner[low + 1] = low + 1, low
    found = []
    for source, target in enumerate(partner):
        for other in range(beside):
            twin = other ^ 1 if (other ^ 1) < beside else other
            place = (source, twin) if target is None else (target, other)
            found.append((source * beside + other, place[0] * beside + place[1]))
    return found


def onward(count):
    return [(source, (source + 1) % count) for source in range(count)]


def vmem_call(body, out_shape, scratch=(), smem=0, inputs=1, cost=None, in_space=VMEM, out_space=VMEM, aliases=None):
    specs = [pl.BlockSpec(memory_space=pltpu.SMEM)] * smem + [pl.BlockSpec(memory_space=in_space)] * inputs
    many = isinstance(out_shape, (list, tuple))
    spaces = out_space if isinstance(out_space, list) else [out_space] * (len(out_shape) if many else 1)
    out_specs = [pl.BlockSpec(memory_space=space) for space in spaces]
    out_specs = out_specs if many else out_specs[0]
    return pl.pallas_call(
        body,
        out_shape=out_shape,
        in_specs=specs,
        out_specs=out_specs,
        scratch_shapes=list(scratch),
        compiler_params=pltpu.CompilerParams(vmem_limit_bytes=24 * 1024 * 1024),
        cost_estimate=cost,
        input_output_aliases=aliases or {},
    )


def blend(parts):
    a, b, c, _, _ = gaussian_taps
    return c * parts[2] + b * (parts[1] + parts[3]) + a * (parts[0] + parts[4])


def prepare_body(masks_hbm, x_hbm, blur_ref, x_ref, masks_ref, sem):
    copies = [
        pltpu.make_async_copy(x_hbm, x_ref, sem.at[0]),
        pltpu.make_async_copy(masks_hbm, masks_ref, sem.at[1]),
    ]
    for copy in copies:
        copy.start()
    span = 2 * TILE
    place, count = lax.axis_index("row"), lax.axis_size("row")
    source = lax.broadcasted_iota(jnp.int32, (LANES, LANES), 0)
    target = lax.broadcasted_iota(jnp.int32, (LANES, LANES), 1)
    outside = jnp.where(source < LANES // 2, source + LANES, source - LANES)

    def held(position):
        low = jnp.logical_or(position >= 0, place > 0)
        return jnp.logical_and(low, jnp.logical_or(position < LANES, place < count - 1))

    for n in range(blur_ref.shape[1] // LANES):
        landing = (target // span + 2 * n) * TILE - RMAX + target % span
        for half, origin in enumerate((source, outside)):
            apart = jnp.abs(origin - landing)
            weight = jnp.zeros((LANES, LANES), jnp.float32)
            for k in range(REACH + 1):
                weight = jnp.where(apart == k, gaussian_taps[REACH + k], weight)
            weight = jnp.where(jnp.logical_and(held(origin), held(landing)), weight, 0.0)
            blur_ref[half * LANES : (half + 1) * LANES, n * LANES : (n + 1) * LANES] = weight
    for copy in copies:
        copy.wait()


def table_body(masks_ref, table_ref, inverse_ref, wide_ref, pair_ref):
    offsets, radii, _ = masks_ref.shape
    wide_ref[...] = jnp.zeros_like(wide_ref)
    wide_ref[0:offsets, :, 0:offsets] = masks_ref[...].astype(jnp.float32)
    total = jnp.zeros((radii, LANES), jnp.float32)
    count = wide_ref.shape[0] // 2
    for k in range(count):
        pair = wide_ref[2 * k] + pltpu.roll(wide_ref[2 * k + 1], 2 * TILE, 1)
        total = total + pair
        pair_ref[k * radii : (k + 1) * radii, :] = pair
    for k in range(count):
        for r in range(radii):
            rows = pair_ref[pl.ds(k * radii + r, TILE, stride=0), :]
            turned = pltpu.roll(rows, 0, 1, stride=1, stride_axis=0)
            table_ref[r * TILE : (r + 1) * TILE, k * LANES : (k + 1) * LANES] = turned.astype(jnp.bfloat16)
    inverse_ref[...] = jnp.broadcast_to(1.0 / jnp.sum(total, axis=1, keepdims=True), (radii, LANES))


def beside(low, high):
    if high is None:
        return low
    lane = lax.broadcasted_iota(jnp.int32, low.shape, 1)
    return jnp.where(lane < LANES // 2, high, low)


def exact_dot(x, y):
    return jnp.dot(x, y, precision=lax.Precision.HIGHEST, preferred_element_type=jnp.float32)


def own_lanes(first, second):
    lane = lax.broadcasted_iota(jnp.int32, first.shape, 1)
    found = pltpu.roll(first, LANES - RMAX, 1)
    found = jnp.where(lane < TILE, found, pltpu.roll(first, LANES - RMAX - TILE, 1))
    found = jnp.where(lane < 2 * TILE, found, pltpu.roll(second, RMAX + TILE, 1))
    return jnp.where(lane < 3 * TILE, found, pltpu.roll(second, RMAX, 1))


def own_body(frames, cols, x_ref, low_ref, high_ref, blur_ref, smooth_ref, pairs_ref, rim_ref, both_ref, found_ref, turn_ref):
    inner = cols - 2 * REACH

    def raw(c):
        rows = pl.ds(c, frames, stride=cols)
        return x_ref[rows, :], beside(low_ref[rows, :], None if high_ref is None else high_ref[rows, :])

    held = {}
    for c in range(cols):
        held[c] = raw(c)
        done = c - REACH
        if done >= REACH:
            for n in range(2):
                both_ref[(done - REACH) * frames : (done - REACH + 1) * frames, n * LANES : (n + 1) * LANES] = blend(
                    [held[done + k][n] for k in range(-REACH, REACH + 1)]
                )
    found_ref[...] = exact_dot(both_ref[...], blur_ref[...])
    turn_ref[...] = jnp.zeros_like(turn_ref)
    lane = lax.broadcasted_iota(jnp.int32, (frames, LANES), 1)
    first = lane < 2 * TILE
    before = None
    for c in range(inner):
        rows = slice(c * frames, (c + 1) * frames)
        value = [found_ref[rows, n * LANES : (n + 1) * LANES] for n in range(2)]
        turn_ref[(c + REACH) * frames : (c + REACH + 1) * frames, :] = own_lanes(*value)
        now = [(v, pltpu.roll(v, 2 * TILE, 1)) for v in value]
        if c == 0 or c == inner - 1:
            for n in range(2):
                rim_ref[0 if c == 0 else 1, n] = value[n]
        if before is not None:
            for n in range(2):
                pairs_ref[2 * n, c - 1] = jnp.where(first, before[n][0], now[n][1]).astype(jnp.bfloat16)
                pairs_ref[2 * n + 1, c - 1] = jnp.where(first, before[n][1], now[n][0]).astype(jnp.bfloat16)
        before = now
    for t in range(frames):
        smooth_ref[t * cols : (t + 1) * cols, :] = turn_ref[pl.ds(t, cols, stride=frames), :].astype(jnp.bfloat16)


def columns_body(frames, cols, x_ref, a_ref, b_ref, c_ref, out_ref, edge_ref):
    place, count = lax.axis_index("space"), lax.axis_size("space")
    phase = lax.rem(place, PHASES)
    lowest, highest = place > 0, place < count - 1
    halo = RMAX + REACH

    def raw(c):
        if 0 <= c < cols:
            return x_ref[pl.ds(c, frames, stride=cols), :]
        at = c + cols if c < 0 else c - cols
        rows = pl.ds(at, frames, stride=cols)
        refs, there = ((c_ref, a_ref, b_ref), lowest) if c < 0 else ((a_ref, b_ref, c_ref), highest)
        value = jnp.where(phase == 0, refs[0][rows, :], jnp.where(phase == 1, refs[1][rows, :], refs[2][rows, :]))
        return jnp.where(there, value, jnp.zeros_like(value))

    order = 0
    for low in (-halo, cols - 2 * REACH):
        held = {}
        for c in range(low, low + halo + 2 * REACH):
            held[c] = raw(c)
            done = c - REACH
            if done >= low + REACH:
                value = blend([held[done + k] for k in range(-REACH, REACH + 1)])
                if done < 0 or done >= cols:
                    value = jnp.where(lowest if done < 0 else highest, value, jnp.zeros_like(value))
                else:
                    slot = done if done < REACH else done - cols + 2 * REACH
                    edge_ref[slot * frames : (slot + 1) * frames, :] = value
                out_ref[order * frames : (order + 1) * frames, :] = value
                order += 1


def placed(frames, cols, edges):
    slots = 2 * REACH
    row = lax.broadcasted_iota(jnp.int32, (frames * cols, slots * frames), 0)
    from_row = lax.broadcasted_iota(jnp.int32, (frames * cols, slots * frames), 1)
    slot, frame = from_row // frames, from_row % frames
    column = jnp.where(slot < REACH, slot, slot + cols - slots)
    pick = jnp.where(row == frame * cols + column, 1.0, 0.0).astype(jnp.bfloat16)
    return jnp.dot(pick, edges, preferred_element_type=jnp.float32).astype(jnp.bfloat16)


def spread_of(smooth):
    wide = LANES // TILE * LANES
    here = lax.broadcasted_iota(jnp.int32, (LANES, wide), 0)
    there = lax.broadcasted_iota(jnp.int32, (LANES, wide), 1)
    wanted = (there // LANES) * TILE + there % TILE
    pick = jnp.where(here == wanted, 1.0, 0.0).astype(jnp.bfloat16)
    return jnp.dot(smooth, pick, preferred_element_type=jnp.float32)


def windows_body(frames, cols, own_ref, low_ref, high_ref, blur_ref, smooth_ref, pairs_ref, rim_ref, tiles_ref, whole_ref, found_ref):
    wide = cols + 2 * RMAX
    edge = RMAX + REACH
    lane = lax.broadcasted_iota(jnp.int32, (frames, LANES), 1)
    first = lane < 2 * TILE
    side = beside(low_ref[...], None if high_ref is None else high_ref[...])
    found_ref[...] = exact_dot(jnp.concatenate([own_ref[...], side], axis=1), blur_ref[...])

    def window(c, n):
        if c == wide:
            return jnp.zeros((frames, LANES), jnp.float32)
        if c == edge or c == wide - edge - 1:
            return rim_ref[0 if c == edge else 1, n]
        at = c if c < edge else c - wide + 2 * edge
        return found_ref[at * frames : (at + 1) * frames, n * LANES : (n + 1) * LANES]

    for begin, end in ((0, edge), (wide - edge - 1, wide)):
        before = None
        for c in range(begin, end + 1):
            now = []
            for n in range(2):
                value = window(c, n)
                now.append((value, pltpu.roll(value, 2 * TILE, 1)))
                if before is not None:
                    low = jnp.where(first, before[n][0], now[n][1])
                    high = jnp.where(first, before[n][1], now[n][0])
                    tiles_ref[2 * n, c - 1] = low.astype(jnp.bfloat16)
                    tiles_ref[2 * n + 1, c - 1] = high.astype(jnp.bfloat16)
            before = now
    for j in range(pairs_ref.shape[0]):
        tiles_ref[j, edge : wide - edge - 1] = pairs_ref[j]
    rows = slice(RMAX * frames, (RMAX + 2 * REACH) * frames)
    edges = own_lanes(found_ref[rows, 0:LANES], found_ref[rows, LANES : 2 * LANES]).astype(jnp.bfloat16)
    whole_ref[...] = smooth_ref[...] + placed(frames, cols, edges)


def inner_span(cols, block):
    edge, last = RMAX + REACH, cols + RMAX - REACH - 2
    return max(0, -(-(edge - 8 * block) // 2)), min(RMAX, (last - 8 * block - 7) // 2) + 1


def times(pieces, weights):
    return lax.dot_general(
        jnp.concatenate(pieces, axis=1), weights, (((1,), (1,)), ((), ())), preferred_element_type=jnp.float32
    )


def inner_body(frames, cols, table_ref, pairs_ref, out_ref):
    tile_count, groups, pitch = out_ref.shape[0], out_ref.shape[1], frames + 8
    for block in range(cols // 8):
        begin, end = inner_span(cols, block)
        start = 8 * block - RMAX - REACH
        pieces = [
            pairs_ref[:, start + 2 * p : start + 2 * p + 8].reshape(tile_count * 8 * frames, LANES)
            for p in range(begin, end)
        ]
        found = times(pieces, table_ref[:, begin * LANES : end * LANES])
        for j in range(tile_count):
            for c in range(8):
                for g in range(groups):
                    row, at = (j * 8 + c) * frames, (8 * block + c) * pitch
                    out_ref[j, g, at : at + frames, :] = found[row : row + frames, g * LANES : (g + 1) * LANES]


def sums_body(frames, cols, table_ref, tiles_ref, inner_ref, out_ref):
    tile_count, groups, pitch = out_ref.shape[0], out_ref.shape[1], frames + 8
    for block in range(cols // 8):
        begin, end = inner_span(cols, block)
        chosen = [p for p in range(RMAX + 1) if not begin <= p < end]
        start = 8 * block
        pieces = [
            tiles_ref[:, start + 2 * p : start + 2 * p + 8].reshape(tile_count * 8 * frames, LANES) for p in chosen
        ]
        weights = [table_ref[:, p * LANES : (p + 1) * LANES] for p in chosen]
        found = times(pieces, jnp.concatenate(weights, axis=1))
        for j in range(tile_count):
            for c in range(8):
                for g in range(groups):
                    row, at = (j * 8 + c) * frames, (8 * block + c) * pitch
                    value = found[row : row + frames, g * LANES : (g + 1) * LANES]
                    out_ref[j, g, at : at + frames, :] = value + inner_ref[j, g, at : at + frames, :]


def correlate_block(frames, cols, n, lags, sources, spread_ref, inverse_ref, total_ref, held):
    groups, pitch, per = total_ref.shape[2], frames + 8, LANES // TILE
    tile_count = len(sources)
    lane = lax.broadcasted_iota(jnp.int32, (8, LANES), 1)
    block = [jnp.logical_and(lane >= TILE * j, lane < TILE * (j + 1)) for j in range(tile_count)]
    c = n * 8
    for j, (found_ref, at) in enumerate(sources):
        totals = {}
        for t in range(frames):
            parts = [found_ref[at, g, pl.ds(c * pitch + t, 8, stride=pitch), :] for g in range(groups)]
            for lag in range(len(lags)):
                row = (MAXLAG - lags[lag]) * cols + c + t * cols
                old = spread_ref[j, pl.ds(pl.multiple_of(row, 8), 8), :]
                for g in range(groups):
                    term = parts[g] * old
                    key = (lag, g)
                    totals[key] = totals[key] + term if key in totals else term
        for lag in range(len(lags)):
            for g in range(groups):
                total_ref[j, lag, g] = totals[(lag, g)]
    for lag in range(len(lags)):
        for g in range(groups):
            pieces = [total_ref[j, lag, g] for j in range(tile_count)]
            for q in range(per):
                joined = None
                for j in range(tile_count):
                    shift = (TILE * (j - q)) % LANES
                    piece = pltpu.roll(pieces[j], shift, 1) if shift else pieces[j]
                    joined = piece if joined is None else jnp.where(block[j], piece, joined)
                r = g * per + q
                held[r, lag] = joined * inverse_ref[r : r + 1, :]


def read_lags(lag_ref):
    return [lag_ref[0, lag] for lag in range(lag_ref.shape[1])]


def products_body(
    frames, cols, table_ref, tiles_ref, inner_ref, whole_ref, earlier_ref, lag_ref, inverse_ref,
    out_ref, spread_ref, held_ref, total_ref,
):
    begun = lax.axis_index("tm") > 0
    rows = frames * cols
    for half, source in enumerate((earlier_ref, whole_ref)):
        value = spread_of(source[...])
        if half == 0:
            value = jnp.where(begun, value, 0.0)
        for j in range(LANES // TILE):
            spread_ref[j, half * rows : (half + 1) * rows, :] = value[:, j * LANES : (j + 1) * LANES]
    sums_body(frames, cols, table_ref, tiles_ref, inner_ref, out_ref)
    lags = read_lags(lag_ref)
    sources = [(out_ref, j) for j in range(out_ref.shape[0])]
    for n in range(held_ref.shape[0]):
        correlate_block(frames, cols, n + 1, lags, sources, spread_ref, inverse_ref, total_ref, held_ref.at[n])


def correlate_body(
    frames, cols, edge_ref, low_ref, high_ref, lag_ref, sums_ref, middle_ref, inverse_ref, given_ref,
    out_ref, spread_ref, held_ref, total_ref, sem,
):
    del given_ref
    blocks = cols // 8

    def send(source, n):
        rows = pl.ds(pl.multiple_of(n * 8, 8), 8)
        return pltpu.make_async_copy(source, out_ref.at[:, :, rows, :], sem.at[n])

    for n in range(blocks - 2):
        send(middle_ref.at[n], n + 1).start()
    tile_count = LANES // TILE
    begun = lax.axis_index("tm") > 0
    side = beside(low_ref[...], None if high_ref is None else high_ref[...])
    place, count = lax.axis_index("row"), lax.axis_size("row")
    spot = lax.broadcasted_iota(jnp.int32, side.shape, 1)
    halo = spot < LANES // 2
    there = jnp.logical_or(jnp.logical_and(halo, place < count - 1), jnp.logical_and(jnp.logical_not(halo), place > 0))
    side = jnp.where(there, side, 0.0)
    shifted = []
    for k in range(-REACH, REACH + 1):
        near, far = edge_ref[...], side
        if k:
            near, far = pltpu.roll(near, (-k) % LANES, 1), pltpu.roll(far, (-k) % LANES, 1)
            near = jnp.where(spot >= LANES - k if k > 0 else spot < -k, far, near)
        shifted.append(near)
    rims = jnp.where(begun, blend(shifted).astype(jnp.bfloat16).astype(jnp.float32), 0.0)
    for j in range(tile_count):
        tile = jnp.where(jnp.logical_and(spot >= TILE * j, spot < TILE * (j + 1)), rims, 0.0)
        shift = TILE
        while shift < LANES:
            tile = tile + pltpu.roll(tile, shift, 1)
            shift *= 2
        for slot in range(2 * REACH):
            column = slot if slot < REACH else slot + cols - 2 * REACH
            spread_ref[j, pl.ds(column, frames, stride=cols), :] = tile[slot * frames : (slot + 1) * frames, :]
    sources = [(sums_ref, j) for j in range(tile_count)]
    lags = read_lags(lag_ref)

    def one_end(end, carry):
        n = end * (blocks - 1)
        correlate_block(frames, cols, n, lags, sources, spread_ref, inverse_ref, total_ref, held_ref.at[end])
        send(held_ref.at[end], n).start()
        return carry

    lax.fori_loop(0, 2, one_end, 0)
    for n in range(blocks):
        send(held_ref.at[0], n).wait()


def local(doppler, cycle_masks, lag_list):
    frames, cols, rows = doppler.shape
    radii = cycle_masks.shape[0]
    lag_count = lag_list.shape[0]
    wide = cols + 2 * RMAX
    edge = RMAX + REACH
    inner = cols - 2 * REACH
    offsets = 2 * RMAX + 1
    tile_count = rows // TILE
    groups = radii * TILE // LANES
    f32, bf16 = jnp.float32, jnp.bfloat16
    shape = jax.ShapeDtypeStruct

    flat = doppler.reshape(frames * cols, rows)
    count, row_count = lax.axis_size("space"), lax.axis_size("row")
    ring = onward(row_count)

    def across(value):
        low = lax.ppermute(value, "row", ring)
        return [low] if row_count == 2 else [low, lax.ppermute(value, "row", [(b, a) for a, b in ring])]

    def across_later(value):
        windows, found = lax.axis_size("tm"), []
        for step in (1,) if row_count == 2 else (1, -1):
            moves = [
                (t * row_count + r, (t + 1) % windows * row_count + (r + step) % row_count)
                for t in range(windows)
                for r in range(row_count)
            ]
            found.append(lax.ppermute(value, ("tm", "row"), moves))
        return found

    def split(refs, lead=1):
        both = 1 if row_count == 2 else 2
        sides = (refs[lead], refs[lead + 1] if both == 2 else None)
        return refs[:lead] + sides + refs[lead + both :]

    one = lax.ppermute(flat, ("space", "row"), pairs(count, 0, row_count))
    two = lax.ppermute(flat, ("space", "row"), pairs(count, 1, row_count))
    three = lax.ppermute(flat, ("space", "row"), pairs(count, 2, row_count))
    near = across(flat)

    depth = (offsets + 1) * 2 * TILE
    masks = jnp.transpose(cycle_masks, (1, 0, 2))
    blur, held, masks = vmem_call(
        prepare_body,
        [
            shape((2 * LANES, 2 * LANES), f32),
            shape((frames * cols, rows), f32),
            shape((offsets, radii, offsets), jnp.int32),
        ],
        scratch=[pltpu.SemaphoreType.DMA((2,))],
        inputs=2,
        in_space=pltpu.HBM,
    )(*[pltpu.with_memory_space_constraint(value, pltpu.HBM) for value in (masks, flat)])

    def own(*refs):
        own_body(frames, cols, *split(refs))

    smooth, inner_pairs, rim = vmem_call(
        own,
        [
            shape((frames * cols, rows), bf16),
            shape((tile_count, inner - 1, frames, LANES), bf16),
            shape((2, 2, frames, LANES), f32),
        ],
        scratch=[
            VMEM((inner * frames, 2 * LANES), f32),
            VMEM((inner * frames, 2 * LANES), f32),
            VMEM((cols * frames, LANES), f32),
        ],
        inputs=2 + len(near),
    )(held, *near, blur)
    later = onward(lax.axis_size("tm"))
    earlier = lax.ppermute(smooth, "tm", later)

    table, inverse = vmem_call(
        table_body,
        [shape((radii * TILE, depth), bf16), shape((radii, LANES), f32)],
        scratch=[VMEM((offsets + 1, radii, LANES), f32), VMEM(((offsets + 1) // 2 * radii, LANES), f32)],
    )(masks)

    sums = shape((tile_count, groups, cols * (frames + 8), LANES), f32)

    def inner_products(*refs):
        inner_body(frames, cols, *refs)

    partial = vmem_call(inner_products, sums, inputs=2)(table, inner_pairs)

    def columns(*refs):
        columns_body(frames, cols, *refs)

    blurred, edges = vmem_call(
        columns, [shape((2 * edge * frames, rows), f32), shape((2 * REACH * frames, rows), f32)], inputs=4
    )(held, one, two, three)

    sides = across(blurred)
    far = across_later(edges)
    edges = lax.ppermute(edges, "tm", later)

    def windows(*refs):
        windows_body(frames, cols, *split(refs))

    tiles, whole = vmem_call(
        windows,
        [shape((tile_count, wide, frames, LANES), bf16), shape((frames * cols, rows), bf16)],
        scratch=[VMEM((2 * edge * frames, 2 * LANES), f32)],
        inputs=5 + len(sides),
    )(blurred, *sides, blur, smooth, inner_pairs, rim)

    blocks = cols // 8
    total = VMEM((tile_count, lag_count, groups, 8, LANES), f32)
    lags = lag_list.reshape(1, lag_count)

    flops = 2 * tile_count * cols * frames * radii * TILE * depth
    cost = pl.CostEstimate(flops=flops, bytes_accessed=1 << 20, transcendentals=0)

    def products(*refs):
        products_body(frames, cols, *refs)

    found, spread, middle = vmem_call(
        products,
        [
            sums,
            shape((tile_count, 2 * frames * cols, LANES), f32),
            shape((blocks - 2, radii, lag_count, 8, LANES), f32),
        ],
        scratch=[total],
        inputs=7,
        cost=cost,
    )(table, tiles, partial, whole, earlier, lags, inverse)

    def correlate(*refs):
        correlate_body(frames, cols, *split(refs))

    out, _ = vmem_call(
        correlate,
        [shape((radii, lag_count, cols, rows), f32), shape(spread.shape, f32)],
        scratch=[
            VMEM((2, radii, lag_count, 8, LANES), f32),
            total,
            pltpu.SemaphoreType.DMA((blocks,)),
        ],
        inputs=6 + len(far),
        out_space=[pl.ANY, VMEM],
        aliases={5 + len(far): 1},
    )(edges, *far, lags, found, middle, inverse, spread)
    return out[None]


def solution(mesh):
    return jax.shard_map(
        local,
        mesh=mesh,
        in_specs=(P("tm", ("patch", "space"), "row"), P(), P()),
        out_specs=P("tm", None, None, ("patch", "space"), "row"),
        check_vma=False,
    )
```

```python
import jax
import jax.numpy as jnp
from jax import lax
from jax.experimental import pallas as pl
from jax.experimental.pallas import tpu as pltpu
from jax.sharding import PartitionSpec as P


RMAX = 16
MAXLAG = 16
TILE = 32

gaussian_taps = (0.05448868, 0.24420134, 0.40261995, 0.24420134, 0.05448868)
REACH = len(gaussian_taps) // 2
LANES = 128
VMEM = pltpu.VMEM
PHASES = 3
END_LANES = 16


def pairs(count, first, beside):
    partner = [None] * count
    for low in range(first, count - 1, PHASES):
        partner[low], partner[low + 1] = low + 1, low
    found = []
    for source, target in enumerate(partner):
        for other in range(beside):
            twin = other ^ 1 if (other ^ 1) < beside else other
            place = (source, twin) if target is None else (target, other)
            found.append((source * beside + other, place[0] * beside + place[1]))
    return found


def onward(count):
    return [(source, (source + 1) % count) for source in range(count)]


def vmem_call(body, out_shape, scratch=(), smem=0, inputs=1, cost=None, in_space=VMEM, out_space=VMEM, aliases=None):
    specs = [pl.BlockSpec(memory_space=pltpu.SMEM)] * smem + [pl.BlockSpec(memory_space=in_space)] * inputs
    many = isinstance(out_shape, (list, tuple))
    spaces = out_space if isinstance(out_space, list) else [out_space] * (len(out_shape) if many else 1)
    out_specs = [pl.BlockSpec(memory_space=space) for space in spaces]
    out_specs = out_specs if many else out_specs[0]
    return pl.pallas_call(
        body,
        out_shape=out_shape,
        in_specs=specs,
        out_specs=out_specs,
        scratch_shapes=list(scratch),
        compiler_params=pltpu.CompilerParams(vmem_limit_bytes=24 * 1024 * 1024),
        cost_estimate=cost,
        input_output_aliases=aliases or {},
    )


def blend(parts):
    a, b, c, _, _ = gaussian_taps
    return c * parts[2] + b * (parts[1] + parts[3]) + a * (parts[0] + parts[4])


def prepare_body(masks_hbm, x_hbm, blur_ref, x_ref, masks_ref, sem):
    copies = [
        pltpu.make_async_copy(x_hbm, x_ref, sem.at[0]),
        pltpu.make_async_copy(masks_hbm, masks_ref, sem.at[1]),
    ]
    for copy in copies:
        copy.start()
    span = 2 * TILE
    place, count = lax.axis_index("row"), lax.axis_size("row")
    source = lax.broadcasted_iota(jnp.int32, (LANES, LANES), 0)
    target = lax.broadcasted_iota(jnp.int32, (LANES, LANES), 1)
    outside = jnp.where(source < LANES // 2, source + LANES, source - LANES)

    def held(position):
        low = jnp.logical_or(position >= 0, place > 0)
        return jnp.logical_and(low, jnp.logical_or(position < LANES, place < count - 1))

    for n in range(blur_ref.shape[1] // LANES):
        landing = (target // span + 2 * n) * TILE - RMAX + target % span
        for half, origin in enumerate((source, outside)):
            apart = jnp.abs(origin - landing)
            weight = jnp.zeros((LANES, LANES), jnp.float32)
            for k in range(REACH + 1):
                weight = jnp.where(apart == k, gaussian_taps[REACH + k], weight)
            weight = jnp.where(jnp.logical_and(held(origin), held(landing)), weight, 0.0)
            blur_ref[half * LANES : (half + 1) * LANES, n * LANES : (n + 1) * LANES] = weight
    for copy in copies:
        copy.wait()


def table_body(masks_ref, table_ref, inverse_ref, wide_ref, pair_ref):
    offsets, radii, _ = masks_ref.shape
    wide_ref[...] = jnp.zeros_like(wide_ref)
    wide_ref[0:offsets, :, 0:offsets] = masks_ref[...].astype(jnp.float32)
    total = jnp.zeros((radii, LANES), jnp.float32)
    count = wide_ref.shape[0] // 2
    for k in range(count):
        pair = wide_ref[2 * k] + pltpu.roll(wide_ref[2 * k + 1], 2 * TILE, 1)
        total = total + pair
        pair_ref[k * radii : (k + 1) * radii, :] = pair
    for k in range(count):
        for r in range(radii):
            rows = pair_ref[pl.ds(k * radii + r, TILE, stride=0), :]
            turned = pltpu.roll(rows, 0, 1, stride=1, stride_axis=0)
            table_ref[r * TILE : (r + 1) * TILE, k * LANES : (k + 1) * LANES] = turned.astype(jnp.bfloat16)
    inverse_ref[...] = jnp.broadcast_to(1.0 / jnp.sum(total, axis=1, keepdims=True), (radii, LANES))


def beside(low, high):
    if high is None:
        return low
    lane = lax.broadcasted_iota(jnp.int32, low.shape, 1)
    return jnp.where(lane < LANES // 2, high, low)


def exact_dot(x, y):
    return jnp.dot(x, y, precision=lax.Precision.HIGHEST, preferred_element_type=jnp.float32)


def own_lanes(first, second):
    lane = lax.broadcasted_iota(jnp.int32, first.shape, 1)
    found = pltpu.roll(first, LANES - RMAX, 1)
    found = jnp.where(lane < TILE, found, pltpu.roll(first, LANES - RMAX - TILE, 1))
    found = jnp.where(lane < 2 * TILE, found, pltpu.roll(second, RMAX + TILE, 1))
    return jnp.where(lane < 3 * TILE, found, pltpu.roll(second, RMAX, 1))


def own_body(frames, cols, x_ref, low_ref, high_ref, blur_ref, smooth_ref, pairs_ref, rim_ref, both_ref, found_ref, turn_ref):
    inner = cols - 2 * REACH

    def raw(c):
        rows = pl.ds(c, frames, stride=cols)
        return x_ref[rows, :], beside(low_ref[rows, :], None if high_ref is None else high_ref[rows, :])

    held = {}
    for c in range(cols):
        held[c] = raw(c)
        done = c - REACH
        if done >= REACH:
            for n in range(2):
                both_ref[(done - REACH) * frames : (done - REACH + 1) * frames, n * LANES : (n + 1) * LANES] = blend(
                    [held[done + k][n] for k in range(-REACH, REACH + 1)]
                )
    found_ref[...] = exact_dot(both_ref[...], blur_ref[...])
    turn_ref[...] = jnp.zeros_like(turn_ref)
    lane = lax.broadcasted_iota(jnp.int32, (frames, LANES), 1)
    first = lane < 2 * TILE
    before = None
    for c in range(inner):
        rows = slice(c * frames, (c + 1) * frames)
        value = [found_ref[rows, n * LANES : (n + 1) * LANES] for n in range(2)]
        turn_ref[(c + REACH) * frames : (c + REACH + 1) * frames, :] = own_lanes(*value)
        now = [(v, pltpu.roll(v, 2 * TILE, 1)) for v in value]
        if c == 0 or c == inner - 1:
            for n in range(2):
                rim_ref[0 if c == 0 else 1, n] = value[n]
        if before is not None:
            for n in range(2):
                pairs_ref[2 * n, c - 1] = jnp.where(first, before[n][0], now[n][1]).astype(jnp.bfloat16)
                pairs_ref[2 * n + 1, c - 1] = jnp.where(first, before[n][1], now[n][0]).astype(jnp.bfloat16)
        before = now
    for t in range(frames):
        smooth_ref[t * cols : (t + 1) * cols, :] = turn_ref[pl.ds(t, cols, stride=frames), :].astype(jnp.bfloat16)


def end_shifts(rows):
    return [(END_LANES // 2 + END_LANES * n) % LANES for n in range(rows // 8)]


def columns_body(frames, cols, x_ref, a_ref, b_ref, c_ref, out_ref, edge_ref, ends_ref):
    place, count = lax.axis_index("space"), lax.axis_size("space")
    phase = lax.rem(place, PHASES)
    lowest, highest = place > 0, place < count - 1
    halo = RMAX + REACH

    def raw(c):
        if 0 <= c < cols:
            return x_ref[pl.ds(c, frames, stride=cols), :]
        at = c + cols if c < 0 else c - cols
        rows = pl.ds(at, frames, stride=cols)
        refs, there = ((c_ref, a_ref, b_ref), lowest) if c < 0 else ((a_ref, b_ref, c_ref), highest)
        value = jnp.where(phase == 0, refs[0][rows, :], jnp.where(phase == 1, refs[1][rows, :], refs[2][rows, :]))
        return jnp.where(there, value, jnp.zeros_like(value))

    order = 0
    for low in (-halo, cols - 2 * REACH):
        held = {}
        for c in range(low, low + halo + 2 * REACH):
            held[c] = raw(c)
            done = c - REACH
            if done >= low + REACH:
                value = blend([held[done + k] for k in range(-REACH, REACH + 1)])
                if done < 0 or done >= cols:
                    value = jnp.where(lowest if done < 0 else highest, value, jnp.zeros_like(value))
                else:
                    slot = done if done < REACH else done - cols + 2 * REACH
                    edge_ref[slot * frames : (slot + 1) * frames, :] = value
                out_ref[order * frames : (order + 1) * frames, :] = value
                order += 1
    spot = lax.broadcasted_iota(jnp.int32, ends_ref.shape, 1)
    ends = jnp.zeros(ends_ref.shape, jnp.float32)
    for n, shift in enumerate(end_shifts(edge_ref.shape[0])):
        ends = jnp.where(spot // END_LANES == n, pltpu.roll(edge_ref[8 * n : 8 * n + 8, :], shift, 1), ends)
    ends_ref[...] = ends


def placed(frames, cols, edges):
    slots = 2 * REACH
    row = lax.broadcasted_iota(jnp.int32, (frames * cols, slots * frames), 0)
    from_row = lax.broadcasted_iota(jnp.int32, (frames * cols, slots * frames), 1)
    slot, frame = from_row // frames, from_row % frames
    column = jnp.where(slot < REACH, slot, slot + cols - slots)
    pick = jnp.where(row == frame * cols + column, 1.0, 0.0).astype(jnp.bfloat16)
    return jnp.dot(pick, edges, preferred_element_type=jnp.float32).astype(jnp.bfloat16)


def spread_of(smooth):
    wide = LANES // TILE * LANES
    here = lax.broadcasted_iota(jnp.int32, (LANES, wide), 0)
    there = lax.broadcasted_iota(jnp.int32, (LANES, wide), 1)
    wanted = (there // LANES) * TILE + there % TILE
    pick = jnp.where(here == wanted, 1.0, 0.0).astype(jnp.bfloat16)
    return jnp.dot(smooth, pick, preferred_element_type=jnp.float32)


def windows_body(frames, cols, own_ref, low_ref, high_ref, blur_ref, smooth_ref, pairs_ref, rim_ref, tiles_ref, whole_ref, found_ref):
    wide = cols + 2 * RMAX
    edge = RMAX + REACH
    lane = lax.broadcasted_iota(jnp.int32, (frames, LANES), 1)
    first = lane < 2 * TILE
    side = beside(low_ref[...], None if high_ref is None else high_ref[...])
    found_ref[...] = exact_dot(jnp.concatenate([own_ref[...], side], axis=1), blur_ref[...])

    def window(c, n):
        if c == wide:
            return jnp.zeros((frames, LANES), jnp.float32)
        if c == edge or c == wide - edge - 1:
            return rim_ref[0 if c == edge else 1, n]
        at = c if c < edge else c - wide + 2 * edge
        return found_ref[at * frames : (at + 1) * frames, n * LANES : (n + 1) * LANES]

    for begin, end in ((0, edge), (wide - edge - 1, wide)):
        before = None
        for c in range(begin, end + 1):
            now = []
            for n in range(2):
                value = window(c, n)
                now.append((value, pltpu.roll(value, 2 * TILE, 1)))
                if before is not None:
                    low = jnp.where(first, before[n][0], now[n][1])
                    high = jnp.where(first, before[n][1], now[n][0])
                    tiles_ref[2 * n, c - 1] = low.astype(jnp.bfloat16)
                    tiles_ref[2 * n + 1, c - 1] = high.astype(jnp.bfloat16)
            before = now
    for j in range(pairs_ref.shape[0]):
        tiles_ref[j, edge : wide - edge - 1] = pairs_ref[j]
    rows = slice(RMAX * frames, (RMAX + 2 * REACH) * frames)
    edges = own_lanes(found_ref[rows, 0:LANES], found_ref[rows, LANES : 2 * LANES]).astype(jnp.bfloat16)
    whole_ref[...] = smooth_ref[...] + placed(frames, cols, edges)


def inner_span(cols, block):
    edge, last = RMAX + REACH, cols + RMAX - REACH - 2
    return max(0, -(-(edge - 8 * block) // 2)), min(RMAX, (last - 8 * block - 7) // 2) + 1


def times(pieces, weights):
    return lax.dot_general(
        jnp.concatenate(pieces, axis=1), weights, (((1,), (1,)), ((), ())), preferred_element_type=jnp.float32
    )


def inner_body(frames, cols, table_ref, pairs_ref, out_ref):
    tile_count, groups, pitch = out_ref.shape[0], out_ref.shape[1], frames + 8
    for block in range(cols // 8):
        begin, end = inner_span(cols, block)
        start = 8 * block - RMAX - REACH
        pieces = [
            pairs_ref[:, start + 2 * p : start + 2 * p + 8].reshape(tile_count * 8 * frames, LANES)
            for p in range(begin, end)
        ]
        found = times(pieces, table_ref[:, begin * LANES : end * LANES])
        for j in range(tile_count):
            for c in range(8):
                for g in range(groups):
                    row, at = (j * 8 + c) * frames, (8 * block + c) * pitch
                    out_ref[j, g, at : at + frames, :] = found[row : row + frames, g * LANES : (g + 1) * LANES]


def sums_body(frames, cols, blocks, table_ref, tiles_ref, inner_ref, out_ref):
    tile_count, groups, pitch = out_ref.shape[0], out_ref.shape[1], frames + 8
    for block in blocks:
        begin, end = inner_span(cols, block)
        chosen = [p for p in range(RMAX + 1) if not begin <= p < end]
        start = 8 * block
        pieces = [
            tiles_ref[:, start + 2 * p : start + 2 * p + 8].reshape(tile_count * 8 * frames, LANES) for p in chosen
        ]
        weights = [table_ref[:, p * LANES : (p + 1) * LANES] for p in chosen]
        found = times(pieces, jnp.concatenate(weights, axis=1))
        for j in range(tile_count):
            for c in range(8):
                for g in range(groups):
                    row, at = (j * 8 + c) * frames, (8 * block + c) * pitch
                    value = found[row : row + frames, g * LANES : (g + 1) * LANES]
                    out_ref[j, g, at : at + frames, :] = value + inner_ref[j, g, at : at + frames, :]


def correlate_block(frames, cols, n, lags, sources, spread_ref, inverse_ref, total_ref, held):
    groups, pitch, per = total_ref.shape[2], frames + 8, LANES // TILE
    tile_count = len(sources)
    lane = lax.broadcasted_iota(jnp.int32, (8, LANES), 1)
    block = [jnp.logical_and(lane >= TILE * j, lane < TILE * (j + 1)) for j in range(tile_count)]
    c = n * 8
    for j, (found_ref, at) in enumerate(sources):
        totals = {}
        for t in range(frames):
            parts = [found_ref[at, g, pl.ds(c * pitch + t, 8, stride=pitch), :] for g in range(groups)]
            for lag in range(len(lags)):
                row = (MAXLAG - lags[lag]) * cols + c + t * cols
                old = spread_ref[j, pl.ds(pl.multiple_of(row, 8), 8), :]
                for g in range(groups):
                    term = parts[g] * old
                    key = (lag, g)
                    totals[key] = totals[key] + term if key in totals else term
        for lag in range(len(lags)):
            for g in range(groups):
                total_ref[j, lag, g] = totals[(lag, g)]
    for lag in range(len(lags)):
        for g in range(groups):
            pieces = [total_ref[j, lag, g] for j in range(tile_count)]
            for q in range(per):
                joined = None
                for j in range(tile_count):
                    shift = (TILE * (j - q)) % LANES
                    piece = pltpu.roll(pieces[j], shift, 1) if shift else pieces[j]
                    joined = piece if joined is None else jnp.where(block[j], piece, joined)
                r = g * per + q
                held[r, lag] = joined * inverse_ref[r : r + 1, :]


def read_lags(lag_ref):
    return [lag_ref[0, lag] for lag in range(lag_ref.shape[1])]


def products_body(
    frames, cols, table_ref, tiles_ref, inner_ref, whole_ref, earlier_ref, lag_ref, inverse_ref,
    out_ref, spread_ref, held_ref, total_ref,
):
    begun = lax.axis_index("tm") > 0
    rows = frames * cols
    for half, source in enumerate((earlier_ref, whole_ref)):
        value = spread_of(source[...])
        if half == 0:
            value = jnp.where(begun, value, 0.0)
        for j in range(LANES // TILE):
            spread_ref[j, half * rows : (half + 1) * rows, :] = value[:, j * LANES : (j + 1) * LANES]
    last = cols // 8 - 1
    sums_body(frames, cols, range(1, last), table_ref, tiles_ref, inner_ref, out_ref)
    lags = read_lags(lag_ref)
    sources = [(out_ref, j) for j in range(out_ref.shape[0])]
    sums_body(frames, cols, (0,), table_ref, tiles_ref, inner_ref, out_ref)
    for n in range(held_ref.shape[0]):
        correlate_block(frames, cols, n + 1, lags, sources, spread_ref, inverse_ref, total_ref, held_ref.at[n])
    sums_body(frames, cols, (last,), table_ref, tiles_ref, inner_ref, out_ref)


def correlate_body(
    frames, cols, edge_ref, low_ref, high_ref, lag_ref, sums_ref, middle_ref, inverse_ref, given_ref,
    out_ref, spread_ref, held_ref, total_ref, sem,
):
    del given_ref
    blocks = cols // 8

    def send(source, n):
        rows = pl.ds(pl.multiple_of(n * 8, 8), 8)
        return pltpu.make_async_copy(source, out_ref.at[:, :, rows, :], sem.at[n])

    for n in range(blocks - 2):
        send(middle_ref.at[n], n + 1).start()
    tile_count = LANES // TILE
    begun = lax.axis_index("tm") > 0
    shifts = end_shifts(edge_ref.shape[0])

    def apart(ends_ref):
        return jnp.concatenate([pltpu.roll(ends_ref[...], LANES - shift, 1) for shift in shifts], axis=0)

    side = beside(apart(low_ref), None if high_ref is None else apart(high_ref))
    place, count = lax.axis_index("row"), lax.axis_size("row")
    spot = lax.broadcasted_iota(jnp.int32, side.shape, 1)
    halo = spot < LANES // 2
    there = jnp.logical_or(jnp.logical_and(halo, place < count - 1), jnp.logical_and(jnp.logical_not(halo), place > 0))
    side = jnp.where(there, side, 0.0)
    shifted = []
    for k in range(-REACH, REACH + 1):
        near, far = edge_ref[...], side
        if k:
            near, far = pltpu.roll(near, (-k) % LANES, 1), pltpu.roll(far, (-k) % LANES, 1)
            near = jnp.where(spot >= LANES - k if k > 0 else spot < -k, far, near)
        shifted.append(near)
    rims = jnp.where(begun, blend(shifted).astype(jnp.bfloat16).astype(jnp.float32), 0.0)
    for j in range(tile_count):
        tile = jnp.where(jnp.logical_and(spot >= TILE * j, spot < TILE * (j + 1)), rims, 0.0)
        shift = TILE
        while shift < LANES:
            tile = tile + pltpu.roll(tile, shift, 1)
            shift *= 2
        for slot in range(2 * REACH):
            column = slot if slot < REACH else slot + cols - 2 * REACH
            spread_ref[j, pl.ds(column, frames, stride=cols), :] = tile[slot * frames : (slot + 1) * frames, :]
    sources = [(sums_ref, j) for j in range(tile_count)]
    lags = read_lags(lag_ref)

    def one_end(end, carry):
        n = end * (blocks - 1)
        correlate_block(frames, cols, n, lags, sources, spread_ref, inverse_ref, total_ref, held_ref.at[end])
        send(held_ref.at[end], n).start()
        return carry

    lax.fori_loop(0, 2, one_end, 0)
    for n in range(blocks):
        send(held_ref.at[0], n).wait()


def local(doppler, cycle_masks, lag_list):
    frames, cols, rows = doppler.shape
    radii = cycle_masks.shape[0]
    lag_count = lag_list.shape[0]
    wide = cols + 2 * RMAX
    edge = RMAX + REACH
    inner = cols - 2 * REACH
    offsets = 2 * RMAX + 1
    tile_count = rows // TILE
    groups = radii * TILE // LANES
    f32, bf16 = jnp.float32, jnp.bfloat16
    shape = jax.ShapeDtypeStruct

    flat = doppler.reshape(frames * cols, rows)
    count, row_count = lax.axis_size("space"), lax.axis_size("row")
    ring = onward(row_count)

    def across(value):
        low = lax.ppermute(value, "row", ring)
        return [low] if row_count == 2 else [low, lax.ppermute(value, "row", [(b, a) for a, b in ring])]

    def across_later(value):
        windows, found = lax.axis_size("tm"), []
        for step in (1,) if row_count == 2 else (1, -1):
            moves = [
                (t * row_count + r, (t + 1) % windows * row_count + (r + step) % row_count)
                for t in range(windows)
                for r in range(row_count)
            ]
            found.append(lax.ppermute(value, ("tm", "row"), moves))
        return found

    def split(refs, lead=1):
        both = 1 if row_count == 2 else 2
        sides = (refs[lead], refs[lead + 1] if both == 2 else None)
        return refs[:lead] + sides + refs[lead + both :]

    one = lax.ppermute(flat, ("space", "row"), pairs(count, 0, row_count))
    two = lax.ppermute(flat, ("space", "row"), pairs(count, 1, row_count))
    three = lax.ppermute(flat, ("space", "row"), pairs(count, 2, row_count))
    near = across(flat)

    depth = (offsets + 1) * 2 * TILE
    masks = jnp.transpose(cycle_masks, (1, 0, 2))
    blur, held, masks = vmem_call(
        prepare_body,
        [
            shape((2 * LANES, 2 * LANES), f32),
            shape((frames * cols, rows), f32),
            shape((offsets, radii, offsets), jnp.int32),
        ],
        scratch=[pltpu.SemaphoreType.DMA((2,))],
        inputs=2,
        in_space=pltpu.HBM,
    )(*[pltpu.with_memory_space_constraint(value, pltpu.HBM) for value in (masks, flat)])

    def own(*refs):
        own_body(frames, cols, *split(refs))

    smooth, inner_pairs, rim = vmem_call(
        own,
        [
            shape((frames * cols, rows), bf16),
            shape((tile_count, inner - 1, frames, LANES), bf16),
            shape((2, 2, frames, LANES), f32),
        ],
        scratch=[
            VMEM((inner * frames, 2 * LANES), f32),
            VMEM((inner * frames, 2 * LANES), f32),
            VMEM((cols * frames, LANES), f32),
        ],
        inputs=2 + len(near),
    )(held, *near, blur)
    later = onward(lax.axis_size("tm"))
    earlier = lax.ppermute(smooth, "tm", later)

    table, inverse = vmem_call(
        table_body,
        [shape((radii * TILE, depth), bf16), shape((radii, LANES), f32)],
        scratch=[VMEM((offsets + 1, radii, LANES), f32), VMEM(((offsets + 1) // 2 * radii + TILE, LANES), f32)],
    )(masks)

    sums = shape((tile_count, groups, cols * (frames + 8), LANES), f32)

    def inner_products(*refs):
        inner_body(frames, cols, *refs)

    partial = vmem_call(inner_products, sums, inputs=2)(table, inner_pairs)

    def columns(*refs):
        columns_body(frames, cols, *refs)

    blurred, edges, ends = vmem_call(
        columns,
        [shape((2 * edge * frames, rows), f32), shape((2 * REACH * frames, rows), f32), shape((8, LANES), f32)],
        inputs=4,
    )(held, one, two, three)

    sides = across(blurred)
    far = across_later(ends)
    edges = lax.ppermute(edges, "tm", later)

    def windows(*refs):
        windows_body(frames, cols, *split(refs))

    tiles, whole = vmem_call(
        windows,
        [shape((tile_count, wide, frames, LANES), bf16), shape((frames * cols, rows), bf16)],
        scratch=[VMEM((2 * edge * frames, 2 * LANES), f32)],
        inputs=5 + len(sides),
    )(blurred, *sides, blur, smooth, inner_pairs, rim)

    blocks = cols // 8
    total = VMEM((tile_count, lag_count, groups, 8, LANES), f32)
    lags = lag_list.reshape(1, lag_count)

    flops = 2 * tile_count * cols * frames * radii * TILE * depth
    cost = pl.CostEstimate(flops=flops, bytes_accessed=1 << 20, transcendentals=0)

    def products(*refs):
        products_body(frames, cols, *refs)

    found, spread, middle = vmem_call(
        products,
        [
            sums,
            shape((tile_count, 2 * frames * cols, LANES), f32),
            shape((blocks - 2, radii, lag_count, 8, LANES), f32),
        ],
        scratch=[total],
        inputs=7,
        cost=cost,
    )(table, tiles, partial, whole, earlier, lags, inverse)

    def correlate(*refs):
        correlate_body(frames, cols, *split(refs))

    out, _ = vmem_call(
        correlate,
        [shape((radii, lag_count, cols, rows), f32), shape(spread.shape, f32)],
        scratch=[
            VMEM((2, radii, lag_count, 8, LANES), f32),
            total,
            pltpu.SemaphoreType.DMA((blocks,)),
        ],
        inputs=6 + len(far),
        out_space=[pl.ANY, VMEM],
        aliases={5 + len(far): 1},
    )(edges, *far, lags, found, middle, inverse, spread)
    return out[None]


def solution(mesh):
    return jax.shard_map(
        local,
        mesh=mesh,
        in_specs=(P("tm", ("patch", "space"), "row"), P(), P()),
        out_specs=P("tm", None, None, ("patch", "space"), "row"),
        check_vma=False,
    )
```

```python
import jax
import jax.numpy as jnp
from jax import lax
from jax.experimental import pallas as pl
from jax.experimental.pallas import tpu as pltpu
from jax.sharding import PartitionSpec as P


RMAX = 16
MAXLAG = 16
TILE = 32

gaussian_taps = (0.05448868, 0.24420134, 0.40261995, 0.24420134, 0.05448868)
REACH = len(gaussian_taps) // 2
LANES = 128
VMEM = pltpu.VMEM
PHASES = 3
END_LANES = 16


def pairs(count, first, beside):
    partner = [None] * count
    for low in range(first, count - 1, PHASES):
        partner[low], partner[low + 1] = low + 1, low
    found = []
    for source, target in enumerate(partner):
        for other in range(beside):
            twin = other ^ 1 if (other ^ 1) < beside else other
            place = (source, twin) if target is None else (target, other)
            found.append((source * beside + other, place[0] * beside + place[1]))
    return found


def onward(count):
    return [(source, (source + 1) % count) for source in range(count)]


def vmem_call(body, out_shape, scratch=(), smem=0, inputs=1, cost=None, in_space=VMEM, out_space=VMEM, aliases=None):
    specs = [pl.BlockSpec(memory_space=pltpu.SMEM)] * smem + [pl.BlockSpec(memory_space=in_space)] * inputs
    many = isinstance(out_shape, (list, tuple))
    spaces = out_space if isinstance(out_space, list) else [out_space] * (len(out_shape) if many else 1)
    out_specs = [pl.BlockSpec(memory_space=space) for space in spaces]
    out_specs = out_specs if many else out_specs[0]
    return pl.pallas_call(
        body,
        out_shape=out_shape,
        in_specs=specs,
        out_specs=out_specs,
        scratch_shapes=list(scratch),
        compiler_params=pltpu.CompilerParams(vmem_limit_bytes=24 * 1024 * 1024),
        cost_estimate=cost,
        input_output_aliases=aliases or {},
    )


def blend(parts):
    a, b, c, _, _ = gaussian_taps
    return c * parts[2] + b * (parts[1] + parts[3]) + a * (parts[0] + parts[4])


def prepare_body(masks_hbm, x_hbm, blur_ref, x_ref, masks_ref, sem):
    copies = [
        pltpu.make_async_copy(x_hbm, x_ref, sem.at[0]),
        pltpu.make_async_copy(masks_hbm, masks_ref, sem.at[1]),
    ]
    for copy in copies:
        copy.start()
    span = 2 * TILE
    place, count = lax.axis_index("row"), lax.axis_size("row")
    source = lax.broadcasted_iota(jnp.int32, (LANES, LANES), 0)
    target = lax.broadcasted_iota(jnp.int32, (LANES, LANES), 1)
    outside = jnp.where(source < LANES // 2, source + LANES, source - LANES)

    def held(position):
        low = jnp.logical_or(position >= 0, place > 0)
        return jnp.logical_and(low, jnp.logical_or(position < LANES, place < count - 1))

    for n in range(blur_ref.shape[1] // LANES):
        landing = (target // span + 2 * n) * TILE - RMAX + target % span
        for half, origin in enumerate((source, outside)):
            apart = jnp.abs(origin - landing)
            weight = jnp.zeros((LANES, LANES), jnp.float32)
            for k in range(REACH + 1):
                weight = jnp.where(apart == k, gaussian_taps[REACH + k], weight)
            weight = jnp.where(jnp.logical_and(held(origin), held(landing)), weight, 0.0)
            blur_ref[half * LANES : (half + 1) * LANES, n * LANES : (n + 1) * LANES] = weight
    for copy in copies:
        copy.wait()


def table_body(masks_ref, table_ref, inverse_ref, wide_ref, pair_ref):
    offsets, radii, _ = masks_ref.shape
    wide_ref[...] = jnp.zeros_like(wide_ref)
    wide_ref[0:offsets, :, 0:offsets] = masks_ref[...].astype(jnp.float32)
    total = jnp.zeros((radii, LANES), jnp.float32)
    count = wide_ref.shape[0] // 2
    for k in range(count):
        pair = wide_ref[2 * k] + pltpu.roll(wide_ref[2 * k + 1], 2 * TILE, 1)
        total = total + pair
        pair_ref[k * radii : (k + 1) * radii, :] = pair
    for k in range(count):
        for r in range(radii):
            rows = pair_ref[pl.ds(k * radii + r, TILE, stride=0), :]
            turned = pltpu.roll(rows, 0, 1, stride=1, stride_axis=0)
            table_ref[r * TILE : (r + 1) * TILE, k * LANES : (k + 1) * LANES] = turned.astype(jnp.bfloat16)
    inverse_ref[...] = jnp.broadcast_to(1.0 / jnp.sum(total, axis=1, keepdims=True), (radii, LANES))


def beside(low, high):
    if high is None:
        return low
    lane = lax.broadcasted_iota(jnp.int32, low.shape, 1)
    return jnp.where(lane < LANES // 2, high, low)


def exact_dot(x, y):
    return jnp.dot(x, y, precision=lax.Precision.HIGHEST, preferred_element_type=jnp.float32)


def own_lanes(first, second):
    lane = lax.broadcasted_iota(jnp.int32, first.shape, 1)
    found = pltpu.roll(first, LANES - RMAX, 1)
    found = jnp.where(lane < TILE, found, pltpu.roll(first, LANES - RMAX - TILE, 1))
    found = jnp.where(lane < 2 * TILE, found, pltpu.roll(second, RMAX + TILE, 1))
    return jnp.where(lane < 3 * TILE, found, pltpu.roll(second, RMAX, 1))


def own_body(frames, cols, x_ref, low_ref, high_ref, blur_ref, smooth_ref, pairs_ref, rim_ref, both_ref, found_ref, turn_ref):
    inner = cols - 2 * REACH

    def raw(c):
        rows = pl.ds(c, frames, stride=cols)
        return x_ref[rows, :], beside(low_ref[rows, :], None if high_ref is None else high_ref[rows, :])

    held = {}
    for c in range(cols):
        held[c] = raw(c)
        done = c - REACH
        if done >= REACH:
            for n in range(2):
                both_ref[(done - REACH) * frames : (done - REACH + 1) * frames, n * LANES : (n + 1) * LANES] = blend(
                    [held[done + k][n] for k in range(-REACH, REACH + 1)]
                )
    found_ref[...] = exact_dot(both_ref[...], blur_ref[...])
    turn_ref[...] = jnp.zeros_like(turn_ref)
    lane = lax.broadcasted_iota(jnp.int32, (frames, LANES), 1)
    first = lane < 2 * TILE
    before = None
    for c in range(inner):
        rows = slice(c * frames, (c + 1) * frames)
        value = [found_ref[rows, n * LANES : (n + 1) * LANES] for n in range(2)]
        turn_ref[(c + REACH) * frames : (c + REACH + 1) * frames, :] = own_lanes(*value)
        now = [(v, pltpu.roll(v, 2 * TILE, 1)) for v in value]
        if c == 0 or c == inner - 1:
            for n in range(2):
                rim_ref[0 if c == 0 else 1, n] = value[n]
        if before is not None:
            for n in range(2):
                pairs_ref[2 * n, RMAX + REACH + c - 1] = jnp.where(first, before[n][0], now[n][1]).astype(jnp.bfloat16)
                pairs_ref[2 * n + 1, RMAX + REACH + c - 1] = jnp.where(first, before[n][1], now[n][0]).astype(jnp.bfloat16)
        before = now
    for t in range(frames):
        smooth_ref[t * cols : (t + 1) * cols, :] = turn_ref[pl.ds(t, cols, stride=frames), :].astype(jnp.bfloat16)


def end_shifts(rows):
    return [(END_LANES // 2 + END_LANES * n) % LANES for n in range(rows // 8)]


def columns_body(frames, cols, x_ref, a_ref, b_ref, c_ref, out_ref, edge_ref, ends_ref):
    place, count = lax.axis_index("space"), lax.axis_size("space")
    phase = lax.rem(place, PHASES)
    lowest, highest = place > 0, place < count - 1
    halo = RMAX + REACH

    def raw(c):
        if 0 <= c < cols:
            return x_ref[pl.ds(c, frames, stride=cols), :]
        at = c + cols if c < 0 else c - cols
        rows = pl.ds(at, frames, stride=cols)
        refs, there = ((c_ref, a_ref, b_ref), lowest) if c < 0 else ((a_ref, b_ref, c_ref), highest)
        value = jnp.where(phase == 0, refs[0][rows, :], jnp.where(phase == 1, refs[1][rows, :], refs[2][rows, :]))
        return jnp.where(there, value, jnp.zeros_like(value))

    order = 0
    for low in (-halo, cols - 2 * REACH):
        held = {}
        for c in range(low, low + halo + 2 * REACH):
            held[c] = raw(c)
            done = c - REACH
            if done >= low + REACH:
                value = blend([held[done + k] for k in range(-REACH, REACH + 1)])
                if done < 0 or done >= cols:
                    value = jnp.where(lowest if done < 0 else highest, value, jnp.zeros_like(value))
                else:
                    slot = done if done < REACH else done - cols + 2 * REACH
                    edge_ref[slot * frames : (slot + 1) * frames, :] = value
                out_ref[order * frames : (order + 1) * frames, :] = value
                order += 1
    spot = lax.broadcasted_iota(jnp.int32, ends_ref.shape, 1)
    ends = jnp.zeros(ends_ref.shape, jnp.float32)
    for n, shift in enumerate(end_shifts(edge_ref.shape[0])):
        ends = jnp.where(spot // END_LANES == n, pltpu.roll(edge_ref[8 * n : 8 * n + 8, :], shift, 1), ends)
    ends_ref[...] = ends


def placed(frames, cols, edges):
    slots = 2 * REACH
    row = lax.broadcasted_iota(jnp.int32, (frames * cols, slots * frames), 0)
    from_row = lax.broadcasted_iota(jnp.int32, (frames * cols, slots * frames), 1)
    slot, frame = from_row // frames, from_row % frames
    column = jnp.where(slot < REACH, slot, slot + cols - slots)
    pick = jnp.where(row == frame * cols + column, 1.0, 0.0).astype(jnp.bfloat16)
    return jnp.dot(pick, edges, preferred_element_type=jnp.float32).astype(jnp.bfloat16)


def spread_of(smooth):
    wide = LANES // TILE * LANES
    here = lax.broadcasted_iota(jnp.int32, (LANES, wide), 0)
    there = lax.broadcasted_iota(jnp.int32, (LANES, wide), 1)
    wanted = (there // LANES) * TILE + there % TILE
    pick = jnp.where(here == wanted, 1.0, 0.0).astype(jnp.bfloat16)
    return jnp.dot(smooth, pick, preferred_element_type=jnp.float32)


def windows_body(frames, cols, own_ref, low_ref, high_ref, blur_ref, smooth_ref, pairs_ref, rim_ref, tiles_ref, whole_ref, found_ref):
    wide = cols + 2 * RMAX
    edge = RMAX + REACH
    lane = lax.broadcasted_iota(jnp.int32, (frames, LANES), 1)
    first = lane < 2 * TILE
    side = beside(low_ref[...], None if high_ref is None else high_ref[...])
    found_ref[...] = exact_dot(jnp.concatenate([own_ref[...], side], axis=1), blur_ref[...])

    def window(c, n):
        if c == wide:
            return jnp.zeros((frames, LANES), jnp.float32)
        if c == edge or c == wide - edge - 1:
            return rim_ref[0 if c == edge else 1, n]
        at = c if c < edge else c - wide + 2 * edge
        return found_ref[at * frames : (at + 1) * frames, n * LANES : (n + 1) * LANES]

    for begin, end in ((0, edge), (wide - edge - 1, wide)):
        before = None
        for c in range(begin, end + 1):
            now = []
            for n in range(2):
                value = window(c, n)
                now.append((value, pltpu.roll(value, 2 * TILE, 1)))
                if before is not None:
                    low = jnp.where(first, before[n][0], now[n][1])
                    high = jnp.where(first, before[n][1], now[n][0])
                    tiles_ref[2 * n, c - 1] = low.astype(jnp.bfloat16)
                    tiles_ref[2 * n + 1, c - 1] = high.astype(jnp.bfloat16)
            before = now
    del pairs_ref
    rows = slice(RMAX * frames, (RMAX + 2 * REACH) * frames)
    edges = own_lanes(found_ref[rows, 0:LANES], found_ref[rows, LANES : 2 * LANES]).astype(jnp.bfloat16)
    whole_ref[...] = smooth_ref[...] + placed(frames, cols, edges)


def inner_span(cols, block):
    edge, last = RMAX + REACH, cols + RMAX - REACH - 2
    return max(0, -(-(edge - 8 * block) // 2)), min(RMAX, (last - 8 * block - 7) // 2) + 1


def times(pieces, weights):
    return lax.dot_general(
        jnp.concatenate(pieces, axis=1), weights, (((1,), (1,)), ((), ())), preferred_element_type=jnp.float32
    )


def inner_body(frames, cols, table_ref, pairs_ref, out_ref):
    tile_count, groups, pitch = out_ref.shape[0], out_ref.shape[1], frames + 8
    for block in range(cols // 8):
        begin, end = inner_span(cols, block)
        start = 8 * block
        pieces = [
            pairs_ref[:, start + 2 * p : start + 2 * p + 8].reshape(tile_count * 8 * frames, LANES)
            for p in range(begin, end)
        ]
        found = times(pieces, table_ref[:, begin * LANES : end * LANES])
        for j in range(tile_count):
            for c in range(8):
                for g in range(groups):
                    row, at = (j * 8 + c) * frames, (8 * block + c) * pitch
                    out_ref[j, g, at : at + frames, :] = found[row : row + frames, g * LANES : (g + 1) * LANES]


def sums_body(frames, cols, blocks, table_ref, tiles_ref, inner_ref, out_ref):
    tile_count, groups, pitch = out_ref.shape[0], out_ref.shape[1], frames + 8
    for block in blocks:
        begin, end = inner_span(cols, block)
        chosen = [p for p in range(RMAX + 1) if not begin <= p < end]
        start = 8 * block
        pieces = [
            tiles_ref[:, start + 2 * p : start + 2 * p + 8].reshape(tile_count * 8 * frames, LANES) for p in chosen
        ]
        weights = [table_ref[:, p * LANES : (p + 1) * LANES] for p in chosen]
        found = times(pieces, jnp.concatenate(weights, axis=1))
        for j in range(tile_count):
            for c in range(8):
                for g in range(groups):
                    row, at = (j * 8 + c) * frames, (8 * block + c) * pitch
                    value = found[row : row + frames, g * LANES : (g + 1) * LANES]
                    out_ref[j, g, at : at + frames, :] = value + inner_ref[j, g, at : at + frames, :]


def correlate_block(frames, cols, n, lags, sources, spread_ref, inverse_ref, total_ref, held):
    groups, pitch, per = total_ref.shape[2], frames + 8, LANES // TILE
    tile_count = len(sources)
    lane = lax.broadcasted_iota(jnp.int32, (8, LANES), 1)
    block = [jnp.logical_and(lane >= TILE * j, lane < TILE * (j + 1)) for j in range(tile_count)]
    c = n * 8
    for j, (found_ref, at) in enumerate(sources):
        totals = {}
        for t in range(frames):
            parts = [found_ref[at, g, pl.ds(c * pitch + t, 8, stride=pitch), :] for g in range(groups)]
            for lag in range(len(lags)):
                row = (MAXLAG - lags[lag]) * cols + c + t * cols
                old = spread_ref[j, pl.ds(pl.multiple_of(row, 8), 8), :]
                for g in range(groups):
                    term = parts[g] * old
                    key = (lag, g)
                    totals[key] = totals[key] + term if key in totals else term
        for lag in range(len(lags)):
            for g in range(groups):
                total_ref[j, lag, g] = totals[(lag, g)]
    for lag in range(len(lags)):
        for g in range(groups):
            pieces = [total_ref[j, lag, g] for j in range(tile_count)]
            for q in range(per):
                joined = None
                for j in range(tile_count):
                    shift = (TILE * (j - q)) % LANES
                    piece = pltpu.roll(pieces[j], shift, 1) if shift else pieces[j]
                    joined = piece if joined is None else jnp.where(block[j], piece, joined)
                r = g * per + q
                held[r, lag] = joined * inverse_ref[r : r + 1, :]


def read_lags(lag_ref):
    return [lag_ref[0, lag] for lag in range(lag_ref.shape[1])]


def products_body(
    frames, cols, table_ref, tiles_ref, inner_ref, whole_ref, earlier_ref, lag_ref, inverse_ref,
    out_ref, spread_ref, held_ref, total_ref,
):
    begun = lax.axis_index("tm") > 0
    rows = frames * cols
    for half, source in enumerate((earlier_ref, whole_ref)):
        value = spread_of(source[...])
        if half == 0:
            value = jnp.where(begun, value, 0.0)
        for j in range(LANES // TILE):
            spread_ref[j, half * rows : (half + 1) * rows, :] = value[:, j * LANES : (j + 1) * LANES]
    last = cols // 8 - 1
    sums_body(frames, cols, range(1, last), table_ref, tiles_ref, inner_ref, out_ref)
    lags = read_lags(lag_ref)
    sources = [(out_ref, j) for j in range(out_ref.shape[0])]
    sums_body(frames, cols, (0,), table_ref, tiles_ref, inner_ref, out_ref)
    for n in range(held_ref.shape[0]):
        correlate_block(frames, cols, n + 1, lags, sources, spread_ref, inverse_ref, total_ref, held_ref.at[n])
    sums_body(frames, cols, (last,), table_ref, tiles_ref, inner_ref, out_ref)


def correlate_body(
    frames, cols, edge_ref, low_ref, high_ref, lag_ref, sums_ref, middle_ref, inverse_ref, given_ref,
    out_ref, spread_ref, held_ref, total_ref, sem,
):
    del given_ref
    blocks = cols // 8

    def send(source, n):
        rows = pl.ds(pl.multiple_of(n * 8, 8), 8)
        return pltpu.make_async_copy(source, out_ref.at[:, :, rows, :], sem.at[n])

    for n in range(blocks - 2):
        send(middle_ref.at[n], n + 1).start()
    tile_count = LANES // TILE
    begun = lax.axis_index("tm") > 0
    shifts = end_shifts(edge_ref.shape[0])

    def apart(ends_ref):
        return jnp.concatenate([pltpu.roll(ends_ref[...], LANES - shift, 1) for shift in shifts], axis=0)

    side = beside(apart(low_ref), None if high_ref is None else apart(high_ref))
    place, count = lax.axis_index("row"), lax.axis_size("row")
    spot = lax.broadcasted_iota(jnp.int32, side.shape, 1)
    halo = spot < LANES // 2
    there = jnp.logical_or(jnp.logical_and(halo, place < count - 1), jnp.logical_and(jnp.logical_not(halo), place > 0))
    side = jnp.where(there, side, 0.0)
    shifted = []
    for k in range(-REACH, REACH + 1):
        near, far = edge_ref[...], side
        if k:
            near, far = pltpu.roll(near, (-k) % LANES, 1), pltpu.roll(far, (-k) % LANES, 1)
            near = jnp.where(spot >= LANES - k if k > 0 else spot < -k, far, near)
        shifted.append(near)
    rims = jnp.where(begun, blend(shifted).astype(jnp.bfloat16).astype(jnp.float32), 0.0)
    for j in range(tile_count):
        tile = jnp.where(jnp.logical_and(spot >= TILE * j, spot < TILE * (j + 1)), rims, 0.0)
        shift = TILE
        while shift < LANES:
            tile = tile + pltpu.roll(tile, shift, 1)
            shift *= 2
        for slot in range(2 * REACH):
            column = slot if slot < REACH else slot + cols - 2 * REACH
            spread_ref[j, pl.ds(column, frames, stride=cols), :] = tile[slot * frames : (slot + 1) * frames, :]
    sources = [(sums_ref, j) for j in range(tile_count)]
    lags = read_lags(lag_ref)

    def one_end(end, carry):
        n = end * (blocks - 1)
        correlate_block(frames, cols, n, lags, sources, spread_ref, inverse_ref, total_ref, held_ref.at[end])
        send(held_ref.at[end], n).start()
        return carry

    lax.fori_loop(0, 2, one_end, 0)
    for n in range(blocks):
        send(held_ref.at[0], n).wait()


def local(doppler, cycle_masks, lag_list):
    frames, cols, rows = doppler.shape
    radii = cycle_masks.shape[0]
    lag_count = lag_list.shape[0]
    wide = cols + 2 * RMAX
    edge = RMAX + REACH
    inner = cols - 2 * REACH
    offsets = 2 * RMAX + 1
    tile_count = rows // TILE
    groups = radii * TILE // LANES
    f32, bf16 = jnp.float32, jnp.bfloat16
    shape = jax.ShapeDtypeStruct

    flat = doppler.reshape(frames * cols, rows)
    count, row_count = lax.axis_size("space"), lax.axis_size("row")
    ring = onward(row_count)

    def across(value):
        low = lax.ppermute(value, "row", ring)
        return [low] if row_count == 2 else [low, lax.ppermute(value, "row", [(b, a) for a, b in ring])]

    def across_later(value):
        windows, found = lax.axis_size("tm"), []
        for step in (1,) if row_count == 2 else (1, -1):
            moves = [
                (t * row_count + r, (t + 1) % windows * row_count + (r + step) % row_count)
                for t in range(windows)
                for r in range(row_count)
            ]
            found.append(lax.ppermute(value, ("tm", "row"), moves))
        return found

    def split(refs, lead=1):
        both = 1 if row_count == 2 else 2
        sides = (refs[lead], refs[lead + 1] if both == 2 else None)
        return refs[:lead] + sides + refs[lead + both :]

    one = lax.ppermute(flat, ("space", "row"), pairs(count, 0, row_count))
    two = lax.ppermute(flat, ("space", "row"), pairs(count, 1, row_count))
    three = lax.ppermute(flat, ("space", "row"), pairs(count, 2, row_count))
    near = across(flat)

    depth = (offsets + 1) * 2 * TILE
    masks = jnp.transpose(cycle_masks, (1, 0, 2))
    blur, held, masks = vmem_call(
        prepare_body,
        [
            shape((2 * LANES, 2 * LANES), f32),
            shape((frames * cols, rows), f32),
            shape((offsets, radii, offsets), jnp.int32),
        ],
        scratch=[pltpu.SemaphoreType.DMA((2,))],
        inputs=2,
        in_space=pltpu.HBM,
    )(*[pltpu.with_memory_space_constraint(value, pltpu.HBM) for value in (masks, flat)])

    def own(*refs):
        own_body(frames, cols, *split(refs))

    smooth, inner_pairs, rim = vmem_call(
        own,
        [
            shape((frames * cols, rows), bf16),
            shape((tile_count, wide, frames, LANES), bf16),
            shape((2, 2, frames, LANES), f32),
        ],
        scratch=[
            VMEM((inner * frames, 2 * LANES), f32),
            VMEM((inner * frames, 2 * LANES), f32),
            VMEM((cols * frames, LANES), f32),
        ],
        inputs=2 + len(near),
    )(held, *near, blur)
    later = onward(lax.axis_size("tm"))
    earlier = lax.ppermute(smooth, "tm", later)

    table, inverse = vmem_call(
        table_body,
        [shape((radii * TILE, depth), bf16), shape((radii, LANES), f32)],
        scratch=[VMEM((offsets + 1, radii, LANES), f32), VMEM(((offsets + 1) // 2 * radii + TILE, LANES), f32)],
    )(masks)

    sums = shape((tile_count, groups, cols * (frames + 8), LANES), f32)

    def inner_products(*refs):
        inner_body(frames, cols, *refs)

    partial = vmem_call(inner_products, sums, inputs=2)(table, inner_pairs)

    def columns(*refs):
        columns_body(frames, cols, *refs)

    blurred, edges, ends = vmem_call(
        columns,
        [shape((2 * edge * frames, rows), f32), shape((2 * REACH * frames, rows), f32), shape((8, LANES), f32)],
        inputs=4,
    )(held, one, two, three)

    sides = across(blurred)
    far = across_later(ends)
    edges = lax.ppermute(edges, "tm", later)

    def windows(*refs):
        windows_body(frames, cols, *split(refs))

    tiles, whole = vmem_call(
        windows,
        [shape((tile_count, wide, frames, LANES), bf16), shape((frames * cols, rows), bf16)],
        scratch=[VMEM((2 * edge * frames, 2 * LANES), f32)],
        inputs=5 + len(sides),
        aliases={3 + len(sides): 0},
    )(blurred, *sides, blur, smooth, inner_pairs, rim)

    blocks = cols // 8
    total = VMEM((tile_count, lag_count, groups, 8, LANES), f32)
    lags = lag_list.reshape(1, lag_count)

    flops = 2 * tile_count * cols * frames * radii * TILE * depth
    cost = pl.CostEstimate(flops=flops, bytes_accessed=1 << 20, transcendentals=0)

    def products(*refs):
        products_body(frames, cols, *refs)

    found, spread, middle = vmem_call(
        products,
        [
            sums,
            shape((tile_count, 2 * frames * cols, LANES), f32),
            shape((blocks - 2, radii, lag_count, 8, LANES), f32),
        ],
        scratch=[total],
        inputs=7,
        cost=cost,
    )(table, tiles, partial, whole, earlier, lags, inverse)

    def correlate(*refs):
        correlate_body(frames, cols, *split(refs))

    out, _ = vmem_call(
        correlate,
        [shape((radii, lag_count, cols, rows), f32), shape(spread.shape, f32)],
        scratch=[
            VMEM((2, radii, lag_count, 8, LANES), f32),
            total,
            pltpu.SemaphoreType.DMA((blocks,)),
        ],
        inputs=6 + len(far),
        out_space=[pl.ANY, VMEM],
        aliases={5 + len(far): 1},
    )(edges, *far, lags, found, middle, inverse, spread)
    return out[None]


def solution(mesh):
    return jax.shard_map(
        local,
        mesh=mesh,
        in_specs=(P("tm", ("patch", "space"), "row"), P(), P()),
        out_specs=P("tm", None, None, ("patch", "space"), "row"),
        check_vma=False,
    )
```
